512 devices in a mesh: gx: 16 (over x, z_hi), gy: 8 (over y, core), gz: 4 (over z_lo).
Axes of the slice: x: 4, y: 4, z: 16 (z_hi: 4, z_lo: 4; z = z_hi * 4 + z_lo), core: 2. Of those that a mesh axis runs over, the one named last changes fastest.
Arguments:
- offsets: float32 [3, 32, 16, 8, 128], P(None, 'gx', 'gy', 'gz'), may hold values from 0 to 1
- velocity: float32 [3, 32, 16, 8, 128], P(None, 'gx', 'gy', 'gz'), may hold values from -3 to 3
- density: float32 [32, 16, 8, 128], P('gx', 'gy', 'gz'), may hold values from 0.98 to 1.02
- mass: float32 [32, 16, 8, 128], P('gx', 'gy', 'gz'), may hold values from 0.008 to 0.024
- occupancy: int32 [32, 16, 8], P('gx', 'gy', 'gz'), may hold values from 32 to 128, as said below
- move_direction: int32 [32, 16, 8, 128], P('gx', 'gy', 'gz'), may hold values from 0 to 2, as said below
- move_slot: int32 [32, 16, 8, 128], P('gx', 'gy', 'gz'), may hold values from 0 to 127, as said below
Outputs:
- position_next: float32 [3, 32, 16, 8, 128], P(None, 'gx', 'gy', 'gz')
- velocity_next: float32 [3, 32, 16, 8, 128], P(None, 'gx', 'gy', 'gz')
- density_next: float32 [32, 16, 8, 128], P('gx', 'gy', 'gz')
- arrivals: float32 [7, 2, 16, 8, 4, 128], P(None, None, 'gx', 'gy', 'gz')
The draws below stay inside these ranges and needn't reach their ends.
Inputs may be any that keep to these rules, and one draw needn't show every extreme that they name: Slots 0 to occupancy - 1 of a cell are live; some cell has all 128 slots live. `move_direction`: 0 on every slot that is not live. `move_slot`: among the live particles of one device with the same nonzero move_direction the slots are distinct, so at most 128 leave a device in one direction; some device sends exactly 128 in one direction. 0 where move_direction is 0.
All inputs are finite; a program needn't handle non-finite values.
Results may differ from the reference program's by a relative error of at most 0.0003.
Values sent between devices are 32-bit elements; how exact they have to be, the bound alone decides.
A program may use at most 64 MiB of HBM per device.

```python
import functools
import math
import jax
import jax.numpy as jnp
from jax import lax

SLOTS = 128
MOVES = 128
CX = 2
CY = 2
CZ = 2
NX = 32
NY = 16
NZ = 8
N_GX = 16
N_GY = 8
N_GZ = 4


def to_grid(values):
    shaped = values.reshape(N_GX, N_GY, N_GZ, CX, CY, CZ, SLOTS)
    shaped = shaped.transpose(0, 3, 1, 4, 2, 5, 6)
    return shaped.reshape(N_GX * CX, N_GY * CY, N_GZ * CZ, SLOTS)


def to_grid_cells(values):
    shaped = values.reshape(N_GX, N_GY, N_GZ, CX, CY, CZ)
    shaped = shaped.transpose(0, 3, 1, 4, 2, 5)
    return shaped.reshape(N_GX * CX, N_GY * CY, N_GZ * CZ)


def layout(key):
    devices_all = N_GX * N_GY * N_GZ
    cells = CX * CY * CZ
    places = cells * SLOTS
    keys = jax.random.split(key, 5)
    counts = jax.random.randint(keys[0], (devices_all * cells,), SLOTS // 4, SLOTS + 1)
    chosen_cell = jax.random.randint(keys[1], (), 0, devices_all * cells)
    counts = jnp.where(jnp.arange(devices_all * cells) == chosen_cell, SLOTS, counts).reshape(devices_all, cells)
    live = (jnp.arange(SLOTS)[None, None, :] < counts[:, :, None]).reshape(devices_all, places)
    leavers = jax.random.randint(keys[2], (devices_all * 2,), MOVES // 4, MOVES + 1)
    chosen_pair = jax.random.randint(keys[3], (), 0, devices_all * 2)
    leavers = jnp.where(jnp.arange(devices_all * 2) == chosen_pair, MOVES, leavers).reshape(devices_all, 2)
    scores = jax.random.randint(keys[4], (devices_all, places), 0, 4096) * places + jnp.arange(places)[None, :]
    scores = jnp.where(live, scores, scores + 4096 * places)
    order = jnp.argsort(scores, axis=1)
    ranking = jnp.argsort(order, axis=1).astype(jnp.int32)
    first = leavers[:, 0:1]
    second = leavers[:, 1:2]
    direction = jnp.where(ranking < first, 1, jnp.where(ranking < first + second, 2, 0)).astype(jnp.int32)
    target = jnp.where(direction == 1, ranking, jnp.where(direction == 2, ranking - first, 0)).astype(jnp.int32)
    return (to_grid_cells(counts).astype(jnp.int32), to_grid(direction), to_grid(target))


def draw_occupancy(key, part):
    return layout(jax.random.fold_in(key, 17))[0]


def draw_move_direction(key, part):
    return layout(jax.random.fold_in(key, 17))[1]


def draw_move_slot(key, part):
    return layout(jax.random.fold_in(key, 17))[2]


def level_of(key, dims, cuts, least, top_value):
    gain, own = 1.0, jax.random.fold_in(key, 6)
    for axis_at, blocks in cuts:
        heights = jnp.exp(jax.random.uniform(jax.random.fold_in(own, axis_at), (blocks,), jnp.float32, least / len(cuts), top_value / len(cuts)))
        gain = gain * jnp.repeat(heights, dims[axis_at] // blocks).reshape([-1 if axis == axis_at else 1 for axis in range(len(dims))])
    return gain


def bell_draw(rng, extent, deviation, reach, cuts=(), held_as=jnp.bfloat16):
    values = deviation * jax.random.normal(rng, extent, jnp.float32)
    if cuts:
        values = values * level_of(rng, extent, cuts, -0.22, 0.18)
    return jnp.clip(values, -reach, reach).astype(held_as)


def setup_inputs(seed: int = 0) -> dict:
    seeds = jax.random.split(jax.random.key(seed), 8)
    return {
        "offsets": jnp.clip(1.0 * jax.random.uniform(seeds[0], (3, NX, NY, NZ, SLOTS), jnp.float32) ** level_of(seeds[0], (3, NX, NY, NZ, SLOTS), ((1, 16), (2, 8), (3, 4)), -0.2, 0.2), 0.0, 1.0),
        "velocity": bell_draw(seeds[1], (3, NX, NY, NZ, SLOTS), 0.5, 3.0, ((1, 16), (2, 8), (3, 4)), jnp.float32),
        "density": jnp.clip(0.98 + 0.03999996 * jax.random.uniform(seeds[2], (NX, NY, NZ, SLOTS), jnp.float32) ** level_of(seeds[2], (NX, NY, NZ, SLOTS), ((0, 16), (1, 8), (2, 4)), -0.2, 0.2), 0.98, 1.02),
        "mass": jnp.clip(jnp.exp(math.log(0.024) - 1.09861225 * jax.random.uniform(seeds[3], (NX, NY, NZ, SLOTS), jnp.float32) ** level_of(seeds[3], (NX, NY, NZ, SLOTS), ((0, 16), (1, 8), (2, 4)), -0.2, 0.2)), 0.008, 0.024),
        "occupancy": draw_occupancy(jax.random.fold_in(seeds[7], 71), 0),
        "move_direction": draw_move_direction(jax.random.fold_in(seeds[7], 71), 0),
        "move_slot": draw_move_slot(jax.random.fold_in(seeds[7], 71), 0),
    }


SMOOTH = 0.5
KERNEL_NORM = 21.0 / (16.0 * math.pi * SMOOTH ** 3)
GRADIENT = 5.0 * KERNEL_NORM / SMOOTH ** 2
SOUND_SPEED = 10.0
STIFFNESS = SOUND_SPEED ** 2 / 7.0
VISCOSITY = 0.1
GRAVITY = 1.0
TIME_STEP = 0.1
HALF_STEP = 0.05

def pair_terms(own, near, shift):
    own_pos, own_vel, own_rho, own_mass = own
    near_pos, near_vel, near_rho, near_mass = near
    own_safe = jnp.where(own_mass > 0, own_rho, 1.0)
    near_safe = jnp.where(near_mass > 0, near_rho, 1.0)
    own_term = STIFFNESS * (own_safe ** 7 - 1.0) / (own_safe * own_safe)
    near_term = STIFFNESS * (near_safe ** 7 - 1.0) / (near_safe * near_safe)
    separation = [own_pos[part][:, :, None] - near_pos[part][:, None, :] - shift[part] for part in range(3)]
    relative = [own_vel[part][:, :, None] - near_vel[part][:, None, :] for part in range(3)]
    dist_sq = separation[0] * separation[0] + separation[1] * separation[1] + separation[2] * separation[2]
    along = relative[0] * separation[0] + relative[1] * separation[1] + relative[2] * separation[2]
    falloff = jnp.maximum(1.0 - 0.5 * jnp.sqrt(dist_sq) / SMOOTH, 0.0)
    weight = -GRADIENT * falloff * falloff * falloff * near_mass[:, None, :]
    closing = jnp.minimum(along, 0.0) / (dist_sq + 0.01 * SMOOTH * SMOOTH)
    viscous = -VISCOSITY * SOUND_SPEED * SMOOTH * closing / (0.5 * (own_safe[:, :, None] + near_safe[:, None, :]))
    push = weight * (own_term[:, :, None] + near_term[:, None, :] + viscous)
    accel = jnp.stack([-lax.optimization_barrier(jnp.sum(push * separation[part], axis=2)) for part in range(3)])
    density_rate = lax.optimization_barrier(jnp.sum(weight * along, axis=2))
    return (accel, density_rate)

def row_rates(block):
    cells_y = block.shape[2] - 2
    cells_z = block.shape[3] - 2
    slots = block.shape[4]
    centre = block[:, 1, 1:-1, 1:-1].reshape(8, -1, slots)
    own = (centre[0:3], centre[3:6], centre[6], centre[7])
    accel = jnp.zeros((3, cells_y * cells_z, slots), jnp.float32)
    density_rate = jnp.zeros((cells_y * cells_z, slots), jnp.float32)
    for shift_x in (-1, 0, 1):
        for shift_y in (-1, 0, 1):
            for shift_z in (-1, 0, 1):
                near = block[:, 1 + shift_x, 1 + shift_y:1 + shift_y + cells_y, 1 + shift_z:1 + shift_z + cells_z]
                near = near.reshape(8, -1, slots)
                part_accel, part_rate = pair_terms(own, (near[0:3], near[3:6], near[6], near[7]), (float(shift_x), float(shift_y), float(shift_z)))
                accel = accel + part_accel
                density_rate = density_rate + part_rate
    accel = accel - jnp.array([0.0, 0.0, GRAVITY], jnp.float32)[:, None, None]
    return (accel.reshape(3, cells_y, cells_z, slots), density_rate.reshape(cells_y, cells_z, slots))

def rates(padded):
    rows = padded.shape[1] - 2

    def one_row(row_index):
        return row_rates(lax.dynamic_slice_in_dim(padded, row_index, 3, 1))
    accel, density_rate = lax.map(one_row, jnp.arange(rows, dtype=jnp.int32))
    return (jnp.moveaxis(accel, 0, 1), density_rate)

def pack_moves(record, direction, target, alive, which, places_out):
    chosen = alive & (direction == which)
    where_to = jnp.where(chosen, target, places_out).astype(jnp.int32)
    summed = jax.ops.segment_sum(record.T, where_to, num_segments=places_out + 1)
    return summed[:places_out].T

def per_device(values):
    leading = values.shape[0]
    shaped = values.reshape(leading, N_GX, CX, N_GY, CY, N_GZ, CZ, SLOTS)
    shaped = shaped.transpose(1, 3, 5, 0, 2, 4, 6, 7)
    return shaped.reshape(N_GX * N_GY * N_GZ, leading, CX * CY * CZ * SLOTS)

def reference(offsets, velocity, density, mass, occupancy, move_direction, move_slot):
    live = jnp.arange(SLOTS, dtype=jnp.int32)[None, None, None, :] < occupancy[..., None]
    carried = jnp.where(live, mass, 0.0)
    fields = jnp.concatenate([offsets, velocity, density[None], carried[None]], 0)
    padding = ((0, 0), (1, 1), (1, 1), (1, 1), (0, 0))
    accel_first, rate_first = rates(jnp.pad(fields, padding))
    half_velocity = velocity + HALF_STEP * accel_first
    half = jnp.concatenate([offsets + HALF_STEP * velocity, half_velocity, (density + HALF_STEP * rate_first)[None], carried[None]], 0)
    accel_second, rate_second = rates(jnp.pad(half, padding))
    new_position = offsets + TIME_STEP * half_velocity
    new_velocity = velocity + TIME_STEP * accel_second
    new_density = density + TIME_STEP * rate_second
    stay = live & (move_direction == 0)
    position_next = jnp.where(stay[None], new_position, 0.0)
    velocity_next = jnp.where(stay[None], new_velocity, 0.0)
    density_next = jnp.where(stay, new_density, 0.0)
    grid_x = (jnp.arange(NX, dtype=jnp.int32) % CX).astype(jnp.float32)[:, None, None, None]
    grid_y = (jnp.arange(NY, dtype=jnp.int32) % CY).astype(jnp.float32)[None, :, None, None]
    grid_z = (jnp.arange(NZ, dtype=jnp.int32) % CZ).astype(jnp.float32)[None, None, :, None]
    shape = density.shape
    block_position = new_position + jnp.stack([jnp.broadcast_to(grid_x, shape), jnp.broadcast_to(grid_y, shape), jnp.broadcast_to(grid_z, shape)])
    record = jnp.concatenate([block_position, new_velocity, new_density[None]], 0)
    down_record = jnp.concatenate([record[0:1] - float(CX), record[1:]], 0)
    up_record = jnp.concatenate([record[0:1] + float(CX), record[1:]], 0)
    flat_dir = per_device(move_direction[None])[:, 0]
    flat_slot = per_device(move_slot[None])[:, 0]
    flat_live = per_device(live[None].astype(jnp.int32))[:, 0] > 0
    pack_down = functools.partial(pack_moves, which=1, places_out=MOVES)
    pack_up = functools.partial(pack_moves, which=2, places_out=MOVES)
    down = jax.vmap(pack_down)(per_device(down_record), flat_dir, flat_slot, flat_live)
    upper = jax.vmap(pack_up)(per_device(up_record), flat_dir, flat_slot, flat_live)
    down = down.reshape(N_GX, N_GY, N_GZ, 7, MOVES)
    upper = upper.reshape(N_GX, N_GY, N_GZ, 7, MOVES)
    zeros_row = jnp.zeros((1, N_GY, N_GZ, 7, MOVES), jnp.float32)
    from_lower = jnp.concatenate([zeros_row, down[:-1]], 0)
    from_upper = jnp.concatenate([upper[1:], zeros_row], 0)
    arrivals = jnp.stack([from_lower, from_upper], 0).transpose(4, 0, 1, 2, 3, 5)
    return (position_next, velocity_next, density_next, arrivals)
```

```python
import math

import jax
import jax.numpy as jnp
from jax import lax
from jax.experimental import pallas as pl
from jax.experimental.pallas import tpu as pltpu
from jax.sharding import PartitionSpec as P

F32 = jnp.float32
BF16 = jnp.bfloat16
MESH = pl.DeviceIdType.MESH
AXES = ("gx", "gy", "gz")
SLOTS = 128

SMOOTH = 0.5
KERNEL_NORM = 21.0 / (16.0 * math.pi * SMOOTH**3)
GRADIENT = 5.0 * KERNEL_NORM / SMOOTH**2
SOUND_SPEED = 10.0
STIFFNESS = SOUND_SPEED**2 / 7.0
TIME_STEP = 0.1
HALF_STEP = 0.05
EPS = 0.01 * SMOOTH * SMOOTH
TINY = 1e-12
CHUNK = 16

REGIONS = [
    (dx, dy, dz)
    for dx in (-1, 0, 1)
    for dy in (-1, 0, 1)
    for dz in (-1, 0, 1)
    if (dx, dy, dz) != (0, 0, 0)
]
SLOT_OF = {region: at for at, region in enumerate(REGIONS)}


def split3(value):
    first = value.astype(BF16).astype(F32)
    rest = value - first
    second = rest.astype(BF16).astype(F32)
    return first, second, rest - second


def row_iota():
    return lax.broadcasted_iota(jnp.int32, (8, SLOTS), 0)


def kernel(
    off_ref, vel_ref, rho_ref, mass_ref, occ_ref, dir_ref, slot_ref,
    pos_out, vel_out, rho_out, arr_out,
    first, half, near_feat, own_feat, near_rows, own_q, own_t, geo, acc, code, fresh, lists, landed,
    send_sem, recv_sem, list_send, list_recv,
):
    place = [lax.axis_index(axis) for axis in AXES]
    count = [lax.axis_size(axis) for axis in AXES]
    row = row_iota()
    lane = lax.broadcasted_iota(jnp.int32, (8, SLOTS), 1)

    first[...] = jnp.zeros_like(first)
    half[...] = jnp.zeros_like(half)
    landed[...] = jnp.zeros_like(landed)

    barrier = pltpu.get_barrier_semaphore()
    greeted = jnp.int32(0)
    for at, axis in enumerate(AXES):
        for step in (-1, 1):
            other = place[at] + step
            there = jnp.logical_and(other >= 0, other < count[at])

            @pl.when(there)
            def _():
                pl.semaphore_signal(barrier, inc=1, device_id={axis: other}, device_id_type=MESH)

            greeted = greeted + there.astype(jnp.int32)

    def halo_copy(phase, region):
        at = max(k for k in range(3) if region[k] != 0)
        buffer = (first, half)[phase]
        source, target = [], []
        for k in range(3):
            span = {-1: 0, 0: pl.ds(1, 2), 1: 3}[region[k]]
            target.append(span)
            source.append({-1: 2, 1: 1}[region[k]] if k == at else span)
        other = lax.rem(place[at] - region[at] + count[at], count[at])
        copy = pltpu.make_async_remote_copy(
            src_ref=buffer.at[tuple(source)],
            dst_ref=buffer.at[tuple(target)],
            send_sem=send_sem.at[phase, SLOT_OF[region]],
            recv_sem=recv_sem.at[phase, SLOT_OF[region]],
            device_id={AXES[at]: other},
            device_id_type=MESH,
        )
        sends = place[at] < count[at] - 1 if region[at] < 0 else place[at] > 0
        receives = place[at] > 0 if region[at] < 0 else place[at] < count[at] - 1
        return copy, sends, receives

    def start(phase, regions):
        for region in regions:
            copy, sends, _ = halo_copy(phase, region)

            @pl.when(sends)
            def _():
                copy.start()

    def wait_in(phase, regions):
        for region in regions:
            copy, _, receives = halo_copy(phase, region)

            @pl.when(receives)
            def _():
                copy.wait_recv()

    def wait_out(phase, regions):
        for region in regions:
            copy, sends, _ = halo_copy(phase, region)

            @pl.when(sends)
            def _():
                copy.wait_send()

    def cell_tile(phase, cx, cy, cz):
        tile = first[cx, cy, cz]
        if phase == 0:
            return tile
        now = half[cx, cy, cz]
        return jnp.concatenate([tile[0:3] + HALF_STEP * tile[3:6], now, tile[7:8]], 0)

    def features(phase, cx, cy, cz, own=None):
        tile = cell_tile(phase, cx, cy, cz)
        shift = jnp.where(row == 0, cx, jnp.where(row == 1, cy, jnp.where(row == 2, cz, 2))) - 2
        moved = tile + shift.astype(F32)
        x, v, rho, m = moved[0:3], moved[3:6], moved[6:7], moved[7:8]
        norm = jnp.sum(x * x, axis=0, keepdims=True)
        cross = jnp.sum(x * v, axis=0, keepdims=True)
        parts = split3(jnp.concatenate([x, v, norm, cross], 0))
        zero = jnp.zeros((8, SLOTS), F32)
        dist, along = [], []
        for at, part in enumerate(parts):
            one = 1.0 if at == 0 else 0.0
            dist.append(jnp.where(row < 3, -2.0 * part, jnp.where(row == 6, one, 0.0)))
            swapped = jnp.concatenate([part[3:6], part[0:3], part[6:8]], 0)
            along.append(jnp.where(row < 6, -swapped, jnp.where(row == 7, one, 0.0)))
        pad = jnp.zeros((5, SLOTS), F32)
        dist_own = jnp.concatenate([part[6:7] for part in parts] + [pad], 0)
        along_own = jnp.concatenate([part[7:8] for part in parts] + [pad], 0)
        cell = cx * 16 + cy * 4 + cz
        for at, (blocks, last) in enumerate(((dist, dist_own), (along, along_own))):
            full = jnp.concatenate(
                [blocks[0], blocks[1], blocks[2], blocks[0], blocks[1], blocks[0], last, zero], 0
            )
            near_feat[cell, :, at * SLOTS : (at + 1) * SLOTS] = full.astype(BF16)
        q = jnp.where(m > 0, rho, 1.0)
        q2 = q * q
        term = STIFFNESS * (q2 * q2 * q2 * q - 1.0) / q2
        near_rows[cell] = jnp.concatenate([x, q, term, m, zero[0:2]], 0)
        if own is not None:
            a, b, c = parts
            ones = jnp.where(row < 3, 1.0, 0.0)
            extra = jnp.concatenate([q, term, zero[0:6]], 0)
            stack = jnp.concatenate([a, a, a, b, b, c, ones, extra], 0).T
            own_feat[own] = stack.astype(BF16)
            rows = pl.ds(pl.multiple_of(own * SLOTS, SLOTS), SLOTS)
            own_q[rows, :] = jnp.broadcast_to(stack[:, 56:57], (SLOTS, SLOTS))
            own_t[rows, :] = jnp.broadcast_to(stack[:, 57:58], (SLOTS, SLOTS))

    def geometry(slot, owns, nears):
        left = jnp.concatenate([own_feat[o] for o in owns], 0) if len(owns) > 1 else own_feat[owns[0]]
        for k, near in enumerate(nears):
            geo[slot, k, 0 : len(owns) * SLOTS, :] = jnp.dot(
                left, near_feat[near], preferred_element_type=F32
            )

    def pairs(slot, owns, nears):
        rows = []
        for near in nears:
            tile = near_rows[near]
            rows.append([jnp.broadcast_to(tile[t : t + 1], (CHUNK, SLOTS)) for t in range(6)])
        for at, o in enumerate(owns):
            for piece in range(0, SLOTS, CHUNK):
                where = pl.ds(pl.multiple_of(o * SLOTS, SLOTS) + piece, CHUNK)
                here = slice(at * SLOTS + piece, at * SLOTS + piece + CHUNK)
                own_qs, own_ts = own_q[where, :], own_t[where, :]
                sums = [acc[t, where, :] for t in range(5)]
                for k in range(len(nears)):
                    x0, x1, x2, q, term, m = rows[k]
                    dist_sq = jnp.maximum(geo[slot, k, here, 0:SLOTS], TINY)
                    along = geo[slot, k, here, SLOTS : 2 * SLOTS]
                    fall = jnp.maximum(1.0 - dist_sq * lax.rsqrt(dist_sq), 0.0)
                    weight = fall * fall * fall * m
                    closing = jnp.minimum(along, 0.0) / ((dist_sq + EPS) * (own_qs + q))
                    push = weight * ((own_ts + term) - closing)
                    sums[0] = sums[0] + push
                    sums[1] = sums[1] + push * x0
                    sums[2] = sums[2] + push * x1
                    sums[3] = sums[3] + push * x2
                    sums[4] = sums[4] + weight * along
                for t in range(5):
                    acc[t, where, :] = sums[t]

    def run_class(steps, plan):
        geometry(0, *plan(0))

        def two(at, carry):
            step = 2 * at
            geometry(1, *plan(step + 1))
            pairs(0, *plan(step))
            geometry(0, *plan(jnp.minimum(step + 2, steps - 1)))
            pairs(1, *plan(step + 1))
            return carry

        lax.fori_loop(0, steps // 2, two, 0)

    def cell_at(cx, cy, cz):
        return cx * 16 + cy * 4 + cz

    def own_plan(step):
        pair, side = step // 2, step % 2
        nears = [cell_at(1 + side, 1 + k // 2, 1 + k % 2) for k in range(4)]
        return [2 * pair, 2 * pair + 1], nears

    def face_plan(axis):
        others = [k for k in range(3) if k != axis]

        def plan(step):
            side, which = step // 2, step % 2
            owns = []
            for last in range(2):
                spot = [None] * 3
                spot[axis], spot[others[0]], spot[others[1]] = side, which, last
                owns.append(spot[0] * 4 + spot[1] * 2 + spot[2])
            nears = []
            for k in range(4):
                spot = [None] * 3
                spot[axis], spot[others[0]], spot[others[1]] = side * 3, 1 + k // 2, 1 + k % 2
                nears.append(cell_at(*spot))
            return owns, nears

        return plan

    def edge_plan(free):
        others = [k for k in range(3) if k != free]

        def plan(step):
            sides = (step // 2, step % 2)
            owns, nears = [], []
            for last in range(2):
                spot = [None] * 3
                spot[others[0]], spot[others[1]], spot[free] = sides[0], sides[1], last
                owns.append(spot[0] * 4 + spot[1] * 2 + spot[2])
                spot[others[0]], spot[others[1]], spot[free] = sides[0] * 3, sides[1] * 3, 1 + last
                nears.append(cell_at(*spot))
            return owns, nears

        return plan

    def corner_plan(step):
        x, y, z = step // 4, (step // 2) % 2, step % 2
        return [step], [cell_at(3 * x, 3 * y, 3 * z)]

    def build(phase, total, spot_of):
        def one(at, carry):
            features(phase, *spot_of(at))
            return carry

        lax.fori_loop(0, total, one, 0)

    def face_spot(axis):
        others = [k for k in range(3) if k != axis]

        def spot(at):
            out = [None] * 3
            out[axis] = (at // 4) * 3
            out[others[0]], out[others[1]] = 1 + (at // 2) % 2, 1 + at % 2
            return out

        return spot

    def edge_spot(free):
        others = [k for k in range(3) if k != free]

        def spot(at):
            out = [None] * 3
            out[others[0]], out[others[1]], out[free] = (at // 4) * 3, ((at // 2) % 2) * 3, 1 + at % 2
            return out

        return spot

    def corner_spot(at):
        return [(at // 4) * 3, ((at // 2) % 2) * 3, (at % 2) * 3]

    def build_own(phase):
        def one(at, carry):
            features(phase, 1 + at // 4, 1 + (at // 2) % 2, 1 + at % 2, own=at)
            return carry

        lax.fori_loop(0, 8, one, 0)

    x_faces = [(-1, 0, 0), (1, 0, 0)]
    y_faces = [(0, -1, 0), (0, 1, 0)]
    z_faces = [(0, 0, -1), (0, 0, 1)]
    xy_edges = [r for r in REGIONS if r[0] and r[1] and not r[2]]
    xz_edges = [r for r in REGIONS if r[0] and not r[1] and r[2]]
    yz_edges = [r for r in REGIONS if not r[0] and r[1] and r[2]]
    corners = [r for r in REGIONS if r[0] and r[1] and r[2]]

    def rates(phase):
        acc[...] = jnp.zeros_like(acc)
        build_own(phase)
        run_class(8, own_plan)
        wait_in(phase, y_faces)
        start(phase, yz_edges)
        build(phase, 8, face_spot(1))
        run_class(4, face_plan(1))
        wait_in(phase, x_faces)
        start(phase, xy_edges + xz_edges)
        wait_in(phase, z_faces)
        build(phase, 8, face_spot(2))
        run_class(4, face_plan(2))
        build(phase, 8, face_spot(0))
        run_class(4, face_plan(0))
        wait_in(phase, xy_edges)
        start(phase, corners)
        wait_in(phase, yz_edges)
        build(phase, 8, edge_spot(0))
        run_class(4, edge_plan(0))
        build(phase, 8, edge_spot(2))
        run_class(4, edge_plan(2))
        wait_in(phase, xz_edges)
        build(phase, 8, edge_spot(1))
        run_class(4, edge_plan(1))
        wait_in(phase, corners)
        build(phase, 8, corner_spot)
        run_class(8, corner_plan)

    def own_rates(o, cx, cy, cz):
        rows = pl.ds(pl.multiple_of(o * SLOTS, SLOTS), SLOTS)
        column = lax.broadcasted_iota(jnp.int32, (SLOTS, SLOTS), 1)
        table = jnp.zeros((SLOTS, SLOTS), F32)
        for t in range(5):
            table = jnp.where(column == t, jnp.sum(acc[t, rows, :], axis=1, keepdims=True), table)
        sums = table.T[0:8]
        x = near_rows[cell_at(cx, cy, cz)][0:3]
        gravity = jnp.where(row == 2, 1.0, 0.0)[0:3]
        accel = GRADIENT * (x * sums[0:1] - sums[1:4]) - gravity
        return accel, -GRADIENT * sums[4:5]

    filled = jnp.zeros((8, SLOTS), jnp.int32)
    for o in range(8):
        filled = jnp.where(row == o, occ_ref[o], filled)
    live = lane < filled
    carried = jnp.where(live, mass_ref[...], 0.0)
    for which in (1, 2):
        chosen = jnp.logical_and(live, dir_ref[...] == which)
        code[which - 1] = jnp.where(chosen, slot_ref[...], -1)
    code[2] = jnp.where(jnp.logical_and(live, dir_ref[...] == 0), 1, 0)
    for o in range(8):
        cx, cy, cz = 1 + o // 4, 1 + (o // 2) % 2, 1 + o % 2
        first[cx, cy, cz] = jnp.concatenate(
            [off_ref[k, o : o + 1] for k in range(3)]
            + [vel_ref[k, o : o + 1] for k in range(3)]
            + [rho_ref[o : o + 1], carried[o : o + 1]],
            0,
        )

    pl.semaphore_wait(barrier, greeted)
    start(0, x_faces + y_faces + z_faces)
    rates(0)

    def to_half(o, carry):
        cx, cy, cz = 1 + o // 4, 1 + (o // 2) % 2, 1 + o % 2
        accel, rate = own_rates(o, cx, cy, cz)
        tile = first[cx, cy, cz]
        half[cx, cy, cz] = jnp.concatenate(
            [tile[3:6] + HALF_STEP * accel, tile[6:7] + HALF_STEP * rate], 0
        )
        return carry

    lax.fori_loop(0, 8, to_half, 0)
    start(1, x_faces + y_faces + z_faces)
    rates(1)

    slots = lax.broadcasted_iota(jnp.int32, (SLOTS, SLOTS), 0)

    def to_new(o, found):
        cx, cy, cz = 1 + o // 4, 1 + (o // 2) % 2, 1 + o % 2
        accel, rate = own_rates(o, cx, cy, cz)
        tile = first[cx, cy, cz]
        new_pos = tile[0:3] + TIME_STEP * half[cx, cy, cz][0:3]
        new_vel = tile[3:6] + TIME_STEP * accel
        new_rho = tile[6:7] + TIME_STEP * rate
        new = jnp.concatenate([new_pos, new_vel, new_rho, jnp.zeros((1, SLOTS), F32)], 0)
        stays = jnp.broadcast_to(code[2, pl.ds(o, 1), :], (8, SLOTS)) > 0
        fresh[o] = jnp.where(stays, new, 0.0)
        spot = jnp.where(row == 0, cx - 1, jnp.where(row == 1, cy - 1, jnp.where(row == 2, cz - 1, 0)))
        record = new + spot.astype(F32)
        out = []
        for which, by in ((0, -2.0), (1, 2.0)):
            parts = split3(record + jnp.where(row == 0, by, 0.0))
            left = jnp.concatenate(parts, 0).astype(BF16)
            target = jnp.broadcast_to(code[which, pl.ds(o, 1), :], (SLOTS, SLOTS))
            chosen = jnp.where(slots == target, 1.0, 0.0).astype(BF16)
            hit = lax.dot_general(
                left, chosen, (((1,), (1,)), ((), ())), preferred_element_type=F32
            )
            out.append(found[which] + hit)
        return tuple(out)

    empty = jnp.zeros((24, SLOTS), F32)
    found = lax.fori_loop(0, 8, to_new, (empty, empty))
    for which in range(2):
        lists[which] = (found[which][0:8] + found[which][8:16]) + found[which][16:24]

    def list_copy(which):
        step = 1 if which == 0 else -1
        other = lax.rem(place[0] + step + count[0], count[0])
        copy = pltpu.make_async_remote_copy(
            src_ref=lists.at[which],
            dst_ref=landed.at[which],
            send_sem=list_send.at[which],
            recv_sem=list_recv.at[which],
            device_id={"gx": other},
            device_id_type=MESH,
        )
        upper, lower = place[0] < count[0] - 1, place[0] > 0
        return copy, (upper, lower)[which], (lower, upper)[which]

    for which in range(2):
        copy, sends, _ = list_copy(which)

        @pl.when(sends)
        def _():
            copy.start()

    for o in range(8):
        tile = fresh[o]
        for k in range(3):
            pos_out[k, o : o + 1, :] = tile[k : k + 1]
            vel_out[k, o : o + 1, :] = tile[3 + k : 4 + k]
        rho_out[o : o + 1, :] = tile[6:7]
    wait_out(0, REGIONS)
    wait_out(1, REGIONS)
    for which in range(2):
        copy, sends, receives = list_copy(which)

        @pl.when(receives)
        def _():
            copy.wait_recv()

        @pl.when(sends)
        def _():
            copy.wait_send()

    for which in range(2):
        tile = landed[which]
        for k in range(7):
            arr_out[2 * k + which : 2 * k + which + 1, :] = tile[k : k + 1]


def body(offsets, velocity, density, mass, occupancy, move_direction, move_slot):
    vmem = pl.BlockSpec(memory_space=pltpu.VMEM)
    smem = pl.BlockSpec(memory_space=pltpu.SMEM)
    pos, vel, rho, arr = pl.pallas_call(
        kernel,
        out_shape=(
            jax.ShapeDtypeStruct((3, 8, SLOTS), F32),
            jax.ShapeDtypeStruct((3, 8, SLOTS), F32),
            jax.ShapeDtypeStruct((8, SLOTS), F32),
            jax.ShapeDtypeStruct((14, SLOTS), F32),
        ),
        in_specs=[vmem, vmem, vmem, vmem, smem, vmem, vmem],
        out_specs=(vmem, vmem, vmem, vmem),
        scratch_shapes=[
            pltpu.VMEM((4, 4, 4, 8, SLOTS), F32),
            pltpu.VMEM((4, 4, 4, 4, SLOTS), F32),
            pltpu.VMEM((64, 64, 2 * SLOTS), BF16),
            pltpu.VMEM((8, SLOTS, 64), BF16),
            pltpu.VMEM((64, 8, SLOTS), F32),
            pltpu.VMEM((8 * SLOTS, SLOTS), F32),
            pltpu.VMEM((8 * SLOTS, SLOTS), F32),
            pltpu.VMEM((2, 4, 2 * SLOTS, 2 * SLOTS), F32),
            pltpu.VMEM((5, 8 * SLOTS, SLOTS), F32),
            pltpu.VMEM((3, 8, SLOTS), jnp.int32),
            pltpu.VMEM((8, 8, SLOTS), F32),
            pltpu.VMEM((2, 8, SLOTS), F32),
            pltpu.VMEM((2, 8, SLOTS), F32),
            pltpu.SemaphoreType.DMA((2, 26)),
            pltpu.SemaphoreType.DMA((2, 26)),
            pltpu.SemaphoreType.DMA((2,)),
            pltpu.SemaphoreType.DMA((2,)),
        ],
        compiler_params=pltpu.CompilerParams(
            collective_id=0, has_side_effects=True, vmem_limit_bytes=48 << 20
        ),
        name="sph_step",
    )(
        offsets.reshape(3, 8, SLOTS),
        velocity.reshape(3, 8, SLOTS),
        density.reshape(8, SLOTS),
        mass.reshape(8, SLOTS),
        occupancy.reshape(8),
        move_direction.reshape(8, SLOTS),
        move_slot.reshape(8, SLOTS),
    )
    return (
        pos.reshape(offsets.shape),
        vel.reshape(velocity.shape),
        rho.reshape(density.shape),
        arr.reshape(7, 2, 1, 1, 1, SLOTS),
    )


def solution(mesh):
    placed = (
        P(None, "gx", "gy", "gz", None),
        P(None, "gx", "gy", "gz", None),
        P("gx", "gy", "gz", None),
        P("gx", "gy", "gz", None),
        P("gx", "gy", "gz"),
        P("gx", "gy", "gz", None),
        P("gx", "gy", "gz", None),
    )
    return jax.shard_map(
        body,
        mesh=mesh,
        in_specs=placed,
        out_specs=(
            P(None, "gx", "gy", "gz", None),
            P(None, "gx", "gy", "gz", None),
            P("gx", "gy", "gz", None),
            P(None, None, "gx", "gy", "gz", None),
        ),
        check_vma=False,
    )
```

```python
import math

import jax
import jax.numpy as jnp
from jax import lax
from jax.experimental import pallas as pl
from jax.experimental.pallas import tpu as pltpu
from jax.sharding import PartitionSpec as P

F32 = jnp.float32
BF16 = jnp.bfloat16
MESH = pl.DeviceIdType.MESH
AXES = ("gx", "gy", "gz")
SLOTS = 128

SMOOTH = 0.5
KERNEL_NORM = 21.0 / (16.0 * math.pi * SMOOTH**3)
GRADIENT = 5.0 * KERNEL_NORM / SMOOTH**2
SOUND_SPEED = 10.0
STIFFNESS = SOUND_SPEED**2 / 7.0
TIME_STEP = 0.1
HALF_STEP = 0.05
EPS = 0.01 * SMOOTH * SMOOTH
TINY = 1e-12
CHUNK = 16

REGIONS = [
    (dx, dy, dz)
    for dx in (-1, 0, 1)
    for dy in (-1, 0, 1)
    for dz in (-1, 0, 1)
    if (dx, dy, dz) != (0, 0, 0)
]
SLOT_OF = {region: at for at, region in enumerate(REGIONS)}


def split3(value):
    first = value.astype(BF16).astype(F32)
    rest = value - first
    second = rest.astype(BF16).astype(F32)
    return first, second, rest - second


def row_iota():
    return lax.broadcasted_iota(jnp.int32, (8, SLOTS), 0)


def kernel(
    off_hbm, vel_hbm, rho_hbm, mass_hbm, occ_ref, dir_hbm, slot_hbm,
    pos_out, vel_out, rho_out, arr_out,
    off_ref, vel_ref, rho_ref, mass_ref, dir_ref, slot_ref,
    first, half, near_feat, own_feat, near_rows, own_q, own_t, geo, acc, code, fresh, lists, landed,
    records, one_hot, load_sem, send_sem, recv_sem, list_send, list_recv,
):
    place = [lax.axis_index(axis) for axis in AXES]
    count = [lax.axis_size(axis) for axis in AXES]
    row = row_iota()
    lane = lax.broadcasted_iota(jnp.int32, (8, SLOTS), 1)

    sources = (off_hbm, vel_hbm, rho_hbm, mass_hbm, dir_hbm, slot_hbm)
    held = (off_ref, vel_ref, rho_ref, mass_ref, dir_ref, slot_ref)
    loads = [
        pltpu.make_async_copy(source, target, load_sem.at[at])
        for at, (source, target) in enumerate(zip(sources, held))
    ]
    for load in loads:
        load.start()

    first[...] = jnp.zeros_like(first)
    half[...] = jnp.zeros_like(half)
    landed[...] = jnp.zeros_like(landed)

    barrier = pltpu.get_barrier_semaphore()
    greeted = jnp.int32(0)
    for at, axis in enumerate(AXES):
        for step in (-1, 1):
            other = place[at] + step
            there = jnp.logical_and(other >= 0, other < count[at])

            @pl.when(there)
            def _():
                pl.semaphore_signal(barrier, inc=1, device_id={axis: other}, device_id_type=MESH)

            greeted = greeted + there.astype(jnp.int32)

    def halo_copy(phase, region):
        at = max(k for k in range(3) if region[k] != 0)
        buffer = (first, half)[phase]
        source, target = [], []
        for k in range(3):
            span = {-1: 0, 0: pl.ds(1, 2), 1: 3}[region[k]]
            target.append(span)
            source.append({-1: 2, 1: 1}[region[k]] if k == at else span)
        other = lax.rem(place[at] - region[at] + count[at], count[at])
        copy = pltpu.make_async_remote_copy(
            src_ref=buffer.at[tuple(source)],
            dst_ref=buffer.at[tuple(target)],
            send_sem=send_sem.at[phase, SLOT_OF[region]],
            recv_sem=recv_sem.at[phase, SLOT_OF[region]],
            device_id={AXES[at]: other},
            device_id_type=MESH,
        )
        sends = place[at] < count[at] - 1 if region[at] < 0 else place[at] > 0
        receives = place[at] > 0 if region[at] < 0 else place[at] < count[at] - 1
        return copy, sends, receives

    def start(phase, regions):
        for region in regions:
            copy, sends, _ = halo_copy(phase, region)

            @pl.when(sends)
            def _():
                copy.start()

    def wait_in(phase, regions):
        for region in regions:
            copy, _, receives = halo_copy(phase, region)

            @pl.when(receives)
            def _():
                copy.wait_recv()

    def wait_out(phase, regions):
        for region in regions:
            copy, sends, _ = halo_copy(phase, region)

            @pl.when(sends)
            def _():
                copy.wait_send()

    def cell_tile(phase, cx, cy, cz):
        tile = first[cx, cy, cz]
        if phase == 0:
            return tile
        now = half[cx, cy, cz]
        return jnp.concatenate([tile[0:3] + HALF_STEP * tile[3:6], now, tile[7:8]], 0)

    def features(phase, cx, cy, cz, own=None):
        tile = cell_tile(phase, cx, cy, cz)
        shift = jnp.where(row == 0, cx, jnp.where(row == 1, cy, jnp.where(row == 2, cz, 2))) - 2
        moved = tile + shift.astype(F32)
        x, v, rho, m = moved[0:3], moved[3:6], moved[6:7], moved[7:8]
        norm = jnp.sum(x * x, axis=0, keepdims=True)
        cross = jnp.sum(x * v, axis=0, keepdims=True)
        parts = split3(jnp.concatenate([x, v, norm, cross], 0))
        zero = jnp.zeros((8, SLOTS), F32)
        dist, along = [], []
        for at, part in enumerate(parts):
            one = 1.0 if at == 0 else 0.0
            dist.append(jnp.where(row < 3, -2.0 * part, jnp.where(row == 6, one, 0.0)))
            swapped = jnp.concatenate([part[3:6], part[0:3], part[6:8]], 0)
            along.append(jnp.where(row < 6, -swapped, jnp.where(row == 7, one, 0.0)))
        pad = jnp.zeros((5, SLOTS), F32)
        dist_own = jnp.concatenate([part[6:7] for part in parts] + [pad], 0)
        along_own = jnp.concatenate([part[7:8] for part in parts] + [pad], 0)
        cell = cx * 16 + cy * 4 + cz
        for at, (blocks, last) in enumerate(((dist, dist_own), (along, along_own))):
            full = jnp.concatenate(
                [blocks[0], blocks[1], blocks[2], blocks[0], blocks[1], blocks[0], last, zero], 0
            )
            near_feat[cell, :, at * SLOTS : (at + 1) * SLOTS] = full.astype(BF16)
        q = jnp.where(m > 0, rho, 1.0)
        q2 = q * q
        term = STIFFNESS * (q2 * q2 * q2 * q - 1.0) / q2
        near_rows[cell] = jnp.concatenate([x, q, term, m, zero[0:2]], 0)
        if own is not None:
            a, b, c = parts
            ones = jnp.where(row < 3, 1.0, 0.0)
            extra = jnp.concatenate([q, term, zero[0:6]], 0)
            stack = jnp.concatenate([a, a, a, b, b, c, ones, extra], 0).T
            own_feat[own] = stack.astype(BF16)
            rows = pl.ds(pl.multiple_of(own * SLOTS, SLOTS), SLOTS)
            own_q[rows, :] = jnp.broadcast_to(stack[:, 56:57], (SLOTS, SLOTS))
            own_t[rows, :] = jnp.broadcast_to(stack[:, 57:58], (SLOTS, SLOTS))

    def geometry(slot, groups):
        at = 0
        for owns, nears in groups:
            left = own_feat[owns[0]]
            if len(owns) > 1:
                left = jnp.concatenate([own_feat[o] for o in owns], 0)
            for near in nears:
                geo[slot, at, 0 : len(owns) * SLOTS, :] = jnp.dot(
                    left, near_feat[near], preferred_element_type=F32
                )
                at += 1

    def pairs(slot, groups):
        base = 0
        for owns, nears in groups:
            rows = []
            for near in nears:
                tile = near_rows[near]
                rows.append([jnp.broadcast_to(tile[t : t + 1], (CHUNK, SLOTS)) for t in range(6)])
            for at, o in enumerate(owns):
                for piece in range(0, SLOTS, CHUNK):
                    where = pl.ds(pl.multiple_of(o * SLOTS, SLOTS) + piece, CHUNK)
                    here = slice(at * SLOTS + piece, at * SLOTS + piece + CHUNK)
                    own_qs, own_ts = own_q[where, :], own_t[where, :]
                    sums = [acc[t, where, :] for t in range(5)]
                    for k in range(len(nears)):
                        x0, x1, x2, q, term, m = rows[k]
                        dist_sq = jnp.maximum(geo[slot, base + k, here, 0:SLOTS], TINY)
                        along = geo[slot, base + k, here, SLOTS : 2 * SLOTS]
                        fall = jnp.maximum(1.0 - dist_sq * lax.rsqrt(dist_sq), 0.0)
                        weight = fall * fall * fall * m
                        closing = jnp.minimum(along, 0.0) / ((dist_sq + EPS) * (own_qs + q))
                        push = weight * ((own_ts + term) - closing)
                        sums[0] = sums[0] + push
                        sums[1] = sums[1] + push * x0
                        sums[2] = sums[2] + push * x1
                        sums[3] = sums[3] + push * x2
                        sums[4] = sums[4] + weight * along
                    for t in range(5):
                        acc[t, where, :] = sums[t]
            base += len(nears)

    def run_class(steps, plan):
        geometry(0, plan(0))

        def two(at, carry):
            step = 2 * at
            geometry(1, plan(step + 1))
            pairs(0, plan(step))
            geometry(0, plan(jnp.minimum(step + 2, steps - 1)))
            pairs(1, plan(step + 1))
            return carry

        lax.fori_loop(0, steps // 2, two, 0)

    def cell_at(cx, cy, cz):
        return cx * 16 + cy * 4 + cz

    def own_plan(step):
        pair, side = step // 2, step % 2
        nears = [cell_at(1 + side, 1 + k // 2, 1 + k % 2) for k in range(4)]
        return [([2 * pair, 2 * pair + 1], nears)]

    def pick(axis, values):
        if isinstance(axis, int):
            return values[axis]
        return jnp.where(axis == 0, values[0], jnp.where(axis == 1, values[1], values[2]))

    OWN, NEAR = (4, 2, 1), (16, 4, 1)

    def face_group(axis, side, which):
        low, high = pick(axis, (1, 0, 0)), pick(axis, (2, 2, 1))
        owns = [
            side * pick(axis, OWN) + which * pick(low, OWN) + last * pick(high, OWN) for last in range(2)
        ]
        nears = [
            side * 3 * pick(axis, NEAR) + (1 + k // 2) * pick(low, NEAR) + (1 + k % 2) * pick(high, NEAR)
            for k in range(4)
        ]
        return owns, nears

    def yz_face_plan(step):
        return [face_group(1 + step // 4, (step // 2) % 2, step % 2)]

    def x_face_plan(step):
        return [face_group(0, step // 2, step % 2)]

    def edge_plan(step):
        free, side = step // 2, step % 2
        low, high = pick(free, (1, 0, 0)), pick(free, (2, 2, 1))
        groups = []
        for other in range(2):
            owns = [
                side * pick(low, OWN) + other * pick(high, OWN) + last * pick(free, OWN)
                for last in range(2)
            ]
            nears = [
                side * 3 * pick(low, NEAR) + other * 3 * pick(high, NEAR) + (1 + last) * pick(free, NEAR)
                for last in range(2)
            ]
            groups.append((owns, nears))
        return groups

    def corner_plan(step):
        return [
            ([step * 4 + k], [cell_at(3 * step, 3 * (k // 2), 3 * (k % 2))]) for k in range(4)
        ]

    def build(phase, total, spot_of):
        def four(at, carry):
            for k in range(4):
                features(phase, *spot_of(4 * at + k))
            return carry

        lax.fori_loop(0, total // 4, four, 0)

    def face_spot(axis):
        others = [k for k in range(3) if k != axis]

        def spot(at):
            out = [None] * 3
            out[axis] = (at // 4) * 3
            out[others[0]], out[others[1]] = 1 + (at // 2) % 2, 1 + at % 2
            return out

        return spot

    def edge_spot(free):
        others = [k for k in range(3) if k != free]

        def spot(at):
            out = [None] * 3
            out[others[0]], out[others[1]], out[free] = (at // 4) * 3, ((at // 2) % 2) * 3, 1 + at % 2
            return out

        return spot

    def corner_spot(at):
        return [(at // 4) * 3, ((at // 2) % 2) * 3, (at % 2) * 3]

    def build_own(phase):
        def two(at, carry):
            for k in range(2):
                o = 2 * at + k
                features(phase, 1 + o // 4, 1 + (o // 2) % 2, 1 + o % 2, own=o)
            return carry

        lax.fori_loop(0, 4, two, 0)

    x_faces = [(-1, 0, 0), (1, 0, 0)]
    y_faces = [(0, -1, 0), (0, 1, 0)]
    z_faces = [(0, 0, -1), (0, 0, 1)]
    xy_edges = [r for r in REGIONS if r[0] and r[1] and not r[2]]
    xz_edges = [r for r in REGIONS if r[0] and not r[1] and r[2]]
    yz_edges = [r for r in REGIONS if not r[0] and r[1] and r[2]]
    corners = [r for r in REGIONS if r[0] and r[1] and r[2]]

    def rates(phase):
        run_class(8, own_plan)
        wait_in(phase, y_faces)
        start(phase, yz_edges)
        build(phase, 8, face_spot(1))
        wait_in(phase, z_faces)
        build(phase, 8, face_spot(2))
        run_class(8, yz_face_plan)
        wait_in(phase, x_faces)
        start(phase, xy_edges + xz_edges)
        build(phase, 8, face_spot(0))
        run_class(4, x_face_plan)
        wait_in(phase, xy_edges)
        start(phase, corners)
        wait_in(phase, yz_edges)
        build(phase, 8, edge_spot(0))
        build(phase, 8, edge_spot(2))
        wait_in(phase, xz_edges)
        build(phase, 8, edge_spot(1))
        run_class(6, edge_plan)
        wait_in(phase, corners)
        build(phase, 8, corner_spot)
        run_class(2, corner_plan)

    def own_rates(o, cx, cy, cz):
        rows = pl.ds(pl.multiple_of(o * SLOTS, SLOTS), SLOTS)
        column = lax.broadcasted_iota(jnp.int32, (SLOTS, SLOTS), 1)
        table = jnp.zeros((SLOTS, SLOTS), F32)
        for t in range(5):
            table = jnp.where(column == t, jnp.sum(acc[t, rows, :], axis=1, keepdims=True), table)
        sums = table.T[0:8]
        x = near_rows[cell_at(cx, cy, cz)][0:3]
        gravity = jnp.where(row == 2, 1.0, 0.0)[0:3]
        accel = GRADIENT * (x * sums[0:1] - sums[1:4]) - gravity
        return accel, -GRADIENT * sums[4:5]

    acc[...] = jnp.zeros_like(acc)
    filled = jnp.zeros((8, SLOTS), jnp.int32)
    for o in range(8):
        filled = jnp.where(row == o, occ_ref[o], filled)
    live = lane < filled
    for load in loads:
        load.wait()
    carried = jnp.where(live, mass_ref[...], 0.0)
    for which in (1, 2):
        chosen = jnp.logical_and(live, dir_ref[...] == which)
        code[which - 1] = jnp.where(chosen, slot_ref[...], -1)
    code[2] = jnp.where(jnp.logical_and(live, dir_ref[...] == 0), 1, 0)
    for o in range(8):
        cx, cy, cz = 1 + o // 4, 1 + (o // 2) % 2, 1 + o % 2
        first[cx, cy, cz] = jnp.concatenate(
            [off_ref[k, o : o + 1] for k in range(3)]
            + [vel_ref[k, o : o + 1] for k in range(3)]
            + [rho_ref[o : o + 1], carried[o : o + 1]],
            0,
        )

    slots = lax.broadcasted_iota(jnp.int32, (SLOTS, SLOTS), 0)
    for which in range(2):
        for o in range(8):
            target = jnp.broadcast_to(code[which, o : o + 1, :], (SLOTS, SLOTS))
            one_hot[which, :, o * SLOTS : (o + 1) * SLOTS] = jnp.where(slots == target, 1.0, 0.0).astype(BF16)
    build_own(0)
    pl.semaphore_wait(barrier, greeted)
    start(0, x_faces + y_faces + z_faces)
    rates(0)

    def to_half(o):
        cx, cy, cz = 1 + o // 4, 1 + (o // 2) % 2, 1 + o % 2
        accel, rate = own_rates(o, cx, cy, cz)
        tile = first[cx, cy, cz]
        half[cx, cy, cz] = jnp.concatenate(
            [tile[3:6] + HALF_STEP * accel, tile[6:7] + HALF_STEP * rate], 0
        )

    def over_own(update):
        def four(at, carry):
            for k in range(4):
                update(4 * at + k)
            return carry

        lax.fori_loop(0, 2, four, 0)

    over_own(to_half)
    start(1, x_faces + y_faces + z_faces)
    acc[...] = jnp.zeros_like(acc)
    build_own(1)
    rates(1)

    def to_new(o):
        cx, cy, cz = 1 + o // 4, 1 + (o // 2) % 2, 1 + o % 2
        accel, rate = own_rates(o, cx, cy, cz)
        tile = first[cx, cy, cz]
        new_pos = tile[0:3] + TIME_STEP * half[cx, cy, cz][0:3]
        new_vel = tile[3:6] + TIME_STEP * accel
        new_rho = tile[6:7] + TIME_STEP * rate
        new = jnp.concatenate([new_pos, new_vel, new_rho, jnp.zeros((1, SLOTS), F32)], 0)
        stays = jnp.broadcast_to(code[2, pl.ds(o, 1), :], (8, SLOTS)) > 0
        fresh[o] = jnp.where(stays, new, 0.0)
        spot = jnp.where(row == 0, cx - 1, jnp.where(row == 1, cy - 1, jnp.where(row == 2, cz - 1, 0)))
        record = new + spot.astype(F32)
        columns = pl.ds(pl.multiple_of(o * SLOTS, SLOTS), SLOTS)
        for which, by in ((0, -2.0), (1, 2.0)):
            parts = split3(record + jnp.where(row == 0, by, 0.0))
            stack = jnp.concatenate([*parts, jnp.zeros((8, SLOTS), F32)], 0)
            records[which, :, columns] = stack.astype(BF16)

    over_own(to_new)
    for which in range(2):
        found = lax.dot_general(
            records[which], one_hot[which], (((1,), (1,)), ((), ())), preferred_element_type=F32
        )
        lists[which] = (found[0:8] + found[8:16]) + found[16:24]

    def list_copy(which):
        step = 1 if which == 0 else -1
        other = lax.rem(place[0] + step + count[0], count[0])
        copy = pltpu.make_async_remote_copy(
            src_ref=lists.at[which],
            dst_ref=landed.at[which],
            send_sem=list_send.at[which],
            recv_sem=list_recv.at[which],
            device_id={"gx": other},
            device_id_type=MESH,
        )
        upper, lower = place[0] < count[0] - 1, place[0] > 0
        return copy, (upper, lower)[which], (lower, upper)[which]

    for which in range(2):
        copy, sends, _ = list_copy(which)

        @pl.when(sends)
        def _():
            copy.start()

    for o in range(8):
        tile = fresh[o]
        for k in range(3):
            pos_out[k, o : o + 1, :] = tile[k : k + 1]
            vel_out[k, o : o + 1, :] = tile[3 + k : 4 + k]
        rho_out[o : o + 1, :] = tile[6:7]
    wait_out(0, REGIONS)
    wait_out(1, REGIONS)
    for which in range(2):
        copy, sends, receives = list_copy(which)

        @pl.when(receives)
        def _():
            copy.wait_recv()

        @pl.when(sends)
        def _():
            copy.wait_send()

    for which in range(2):
        tile = landed[which]
        for k in range(7):
            arr_out[2 * k + which : 2 * k + which + 1, :] = tile[k : k + 1]


def body(offsets, velocity, density, mass, occupancy, move_direction, move_slot):
    vmem = pl.BlockSpec(memory_space=pltpu.VMEM)
    smem = pl.BlockSpec(memory_space=pltpu.SMEM)
    hbm = pl.BlockSpec(memory_space=pl.ANY)
    pos, vel, rho, arr = pl.pallas_call(
        kernel,
        out_shape=(
            jax.ShapeDtypeStruct((3, 8, SLOTS), F32),
            jax.ShapeDtypeStruct((3, 8, SLOTS), F32),
            jax.ShapeDtypeStruct((8, SLOTS), F32),
            jax.ShapeDtypeStruct((14, SLOTS), F32),
        ),
        in_specs=[hbm, hbm, hbm, hbm, smem, hbm, hbm],
        out_specs=(vmem, vmem, vmem, vmem),
        scratch_shapes=[
            pltpu.VMEM((3, 8, SLOTS), F32),
            pltpu.VMEM((3, 8, SLOTS), F32),
            pltpu.VMEM((8, SLOTS), F32),
            pltpu.VMEM((8, SLOTS), F32),
            pltpu.VMEM((8, SLOTS), jnp.int32),
            pltpu.VMEM((8, SLOTS), jnp.int32),
            pltpu.VMEM((4, 4, 4, 8, SLOTS), F32),
            pltpu.VMEM((4, 4, 4, 4, SLOTS), F32),
            pltpu.VMEM((64, 64, 2 * SLOTS), BF16),
            pltpu.VMEM((8, SLOTS, 64), BF16),
            pltpu.VMEM((64, 8, SLOTS), F32),
            pltpu.VMEM((8 * SLOTS, SLOTS), F32),
            pltpu.VMEM((8 * SLOTS, SLOTS), F32),
            pltpu.VMEM((2, 4, 2 * SLOTS, 2 * SLOTS), F32),
            pltpu.VMEM((5, 8 * SLOTS, SLOTS), F32),
            pltpu.VMEM((3, 8, SLOTS), jnp.int32),
            pltpu.VMEM((8, 8, SLOTS), F32),
            pltpu.VMEM((2, 8, SLOTS), F32),
            pltpu.VMEM((2, 8, SLOTS), F32),
            pltpu.VMEM((2, 32, 8 * SLOTS), BF16),
            pltpu.VMEM((2, SLOTS, 8 * SLOTS), BF16),
            pltpu.SemaphoreType.DMA((6,)),
            pltpu.SemaphoreType.DMA((2, 26)),
            pltpu.SemaphoreType.DMA((2, 26)),
            pltpu.SemaphoreType.DMA((2,)),
            pltpu.SemaphoreType.DMA((2,)),
        ],
        compiler_params=pltpu.CompilerParams(
            collective_id=0, has_side_effects=True, vmem_limit_bytes=67_043_328
        ),
        name="sph_step",
    )(
        offsets.reshape(3, 8, SLOTS),
        velocity.reshape(3, 8, SLOTS),
        density.reshape(8, SLOTS),
        mass.reshape(8, SLOTS),
        occupancy.reshape(8),
        move_direction.reshape(8, SLOTS),
        move_slot.reshape(8, SLOTS),
    )
    return (
        pos.reshape(offsets.shape),
        vel.reshape(velocity.shape),
        rho.reshape(density.shape),
        arr.reshape(7, 2, 1, 1, 1, SLOTS),
    )


def solution(mesh):
    placed = (
        P(None, "gx", "gy", "gz", None),
        P(None, "gx", "gy", "gz", None),
        P("gx", "gy", "gz", None),
        P("gx", "gy", "gz", None),
        P("gx", "gy", "gz"),
        P("gx", "gy", "gz", None),
        P("gx", "gy", "gz", None),
    )
    return jax.shard_map(
        body,
        mesh=mesh,
        in_specs=placed,
        out_specs=(
            P(None, "gx", "gy", "gz", None),
            P(None, "gx", "gy", "gz", None),
            P("gx", "gy", "gz", None),
            P(None, None, "gx", "gy", "gz", None),
        ),
        check_vma=False,
    )
```

```python
import math

import jax
import jax.numpy as jnp
from jax import lax
from jax.experimental import pallas as pl
from jax.experimental.pallas import tpu as pltpu
from jax.sharding import PartitionSpec as P

F32 = jnp.float32
BF16 = jnp.bfloat16
MESH = pl.DeviceIdType.MESH
AXES = ("gx", "gy", "gz")
SLOTS = 128

SMOOTH = 0.5
KERNEL_NORM = 21.0 / (16.0 * math.pi * SMOOTH**3)
GRADIENT = 5.0 * KERNEL_NORM / SMOOTH**2
SOUND_SPEED = 10.0
STIFFNESS = SOUND_SPEED**2 / 7.0
TIME_STEP = 0.1
HALF_STEP = 0.05
EPS = 0.01 * SMOOTH * SMOOTH
TINY = 1e-12
CHUNK = 16

REGIONS = [
    (dx, dy, dz)
    for dx in (-1, 0, 1)
    for dy in (-1, 0, 1)
    for dz in (-1, 0, 1)
    if (dx, dy, dz) != (0, 0, 0)
]
SLOT_OF = {region: at for at, region in enumerate(REGIONS)}


def split3(value):
    first = value.astype(BF16).astype(F32)
    rest = value - first
    second = rest.astype(BF16).astype(F32)
    return first, second, rest - second


def row_iota():
    return lax.broadcasted_iota(jnp.int32, (8, SLOTS), 0)


def kernel(
    off_hbm, vel_hbm, rho_hbm, mass_hbm, occ_hbm, dir_hbm, slot_hbm,
    pos_out, vel_out, rho_out, arr_out,
    off_ref, vel_ref, rho_ref, mass_ref, occ_ref, dir_ref, slot_ref,
    first, half, near_feat, own_feat, near_rows, own_q, own_t, geo, acc, code, fresh, lists, landed,
    records, one_hot, load_sem, send_sem, recv_sem, list_send, list_recv,
):
    place = [lax.axis_index(axis) for axis in AXES]
    count = [lax.axis_size(axis) for axis in AXES]
    row = row_iota()
    lane = lax.broadcasted_iota(jnp.int32, (8, SLOTS), 1)

    sources = (off_hbm, vel_hbm, rho_hbm, mass_hbm, occ_hbm, dir_hbm, slot_hbm)
    held = (off_ref, vel_ref, rho_ref, mass_ref, occ_ref, dir_ref, slot_ref)
    loads = [
        pltpu.make_async_copy(source, target, load_sem.at[at])
        for at, (source, target) in enumerate(zip(sources, held))
    ]
    for load in loads:
        load.start()

    first[...] = jnp.zeros_like(first)
    half[...] = jnp.zeros_like(half)
    landed[...] = jnp.zeros_like(landed)

    barrier = pltpu.get_barrier_semaphore()
    greeted = jnp.int32(0)
    for at, axis in enumerate(AXES):
        for step in (-1, 1):
            other = place[at] + step
            there = jnp.logical_and(other >= 0, other < count[at])

            @pl.when(there)
            def _():
                pl.semaphore_signal(barrier, inc=1, device_id={axis: other}, device_id_type=MESH)

            greeted = greeted + there.astype(jnp.int32)

    def halo_copy(phase, region):
        at = max(k for k in range(3) if region[k] != 0)
        buffer = (first, half)[phase]
        source, target = [], []
        for k in range(3):
            span = {-1: 0, 0: pl.ds(1, 2), 1: 3}[region[k]]
            target.append(span)
            source.append({-1: 2, 1: 1}[region[k]] if k == at else span)
        other = lax.rem(place[at] - region[at] + count[at], count[at])
        copy = pltpu.make_async_remote_copy(
            src_ref=buffer.at[tuple(source)],
            dst_ref=buffer.at[tuple(target)],
            send_sem=send_sem.at[phase, SLOT_OF[region]],
            recv_sem=recv_sem.at[phase, SLOT_OF[region]],
            device_id={AXES[at]: other},
            device_id_type=MESH,
        )
        sends = place[at] < count[at] - 1 if region[at] < 0 else place[at] > 0
        receives = place[at] > 0 if region[at] < 0 else place[at] < count[at] - 1
        return copy, sends, receives

    def start(phase, regions):
        for region in regions:
            copy, sends, _ = halo_copy(phase, region)

            @pl.when(sends)
            def _():
                copy.start()

    def wait_in(phase, regions):
        for region in regions:
            copy, _, receives = halo_copy(phase, region)

            @pl.when(receives)
            def _():
                copy.wait_recv()

    def wait_out(phase, regions):
        for region in regions:
            copy, sends, _ = halo_copy(phase, region)

            @pl.when(sends)
            def _():
                copy.wait_send()

    def cell_tile(phase, cx, cy, cz):
        tile = first[cx, cy, cz]
        if phase == 0:
            return tile
        now = half[cx, cy, cz]
        return jnp.concatenate([tile[0:3] + HALF_STEP * tile[3:6], now, tile[7:8]], 0)

    def features(phase, cx, cy, cz, own=None):
        tile = cell_tile(phase, cx, cy, cz)
        shift = jnp.where(row == 0, cx, jnp.where(row == 1, cy, jnp.where(row == 2, cz, 2))) - 2
        moved = tile + shift.astype(F32)
        x, v, rho, m = moved[0:3], moved[3:6], moved[6:7], moved[7:8]
        norm = jnp.sum(x * x, axis=0, keepdims=True)
        cross = jnp.sum(x * v, axis=0, keepdims=True)
        parts = split3(jnp.concatenate([x, v, norm, cross], 0))
        zero = jnp.zeros((8, SLOTS), F32)
        dist, along = [], []
        for at, part in enumerate(parts):
            one = 1.0 if at == 0 else 0.0
            dist.append(jnp.where(row < 3, -2.0 * part, jnp.where(row == 6, one, 0.0)))
            swapped = jnp.concatenate([part[3:6], part[0:3], part[6:8]], 0)
            along.append(jnp.where(row < 6, -swapped, jnp.where(row == 7, one, 0.0)))
        pad = jnp.zeros((5, SLOTS), F32)
        dist_own = jnp.concatenate([part[6:7] for part in parts] + [pad], 0)
        along_own = jnp.concatenate([part[7:8] for part in parts] + [pad], 0)
        cell = cx * 16 + cy * 4 + cz
        for at, (blocks, last) in enumerate(((dist, dist_own), (along, along_own))):
            full = jnp.concatenate(
                [blocks[0], blocks[1], blocks[2], blocks[0], blocks[1], blocks[0], last, zero], 0
            )
            near_feat[cell, :, at * SLOTS : (at + 1) * SLOTS] = full.astype(BF16)
        q = jnp.where(m > 0, rho, 1.0)
        q2 = q * q
        term = STIFFNESS * (q2 * q2 * q2 * q - 1.0) / q2
        near_rows[cell] = jnp.concatenate([x, q, term, m, zero[0:2]], 0)
        if own is not None:
            a, b, c = parts
            ones = jnp.where(row < 3, 1.0, 0.0)
            extra = jnp.concatenate([q, term, zero[0:6]], 0)
            stack = jnp.concatenate([a, a, a, b, b, c, ones, extra], 0).T
            own_feat[own] = stack.astype(BF16)
            rows = pl.ds(pl.multiple_of(own * SLOTS, SLOTS), SLOTS)
            own_q[rows, :] = jnp.broadcast_to(stack[:, 56:57], (SLOTS, SLOTS))
            own_t[rows, :] = jnp.broadcast_to(stack[:, 57:58], (SLOTS, SLOTS))

    def products(slot, groups):
        made, at = [], 0
        for owns, nears in groups:
            for near in nears:

                def make(owns=owns, near=near, at=at):
                    left = own_feat[owns[0]]
                    if len(owns) > 1:
                        left = jnp.concatenate([own_feat[o] for o in owns], 0)
                    geo[slot, at, 0 : len(owns) * SLOTS, :] = jnp.dot(
                        left, near_feat[near], preferred_element_type=F32
                    )

                made.append(make)
                at += 1
        return made

    def add_pairs(slot, base, owns, nears, at, piece):
        o = owns[at]
        where = pl.ds(pl.multiple_of(o * SLOTS, SLOTS) + piece, CHUNK)
        here = slice(at * SLOTS + piece, at * SLOTS + piece + CHUNK)
        own_qs, own_ts = own_q[where, :], own_t[where, :]
        sums = [acc[t, where, :] for t in range(5)]
        for k, near in enumerate(nears):
            x0, x1, x2, q, term, m = [near_rows[near, pl.ds(t, CHUNK, stride=0), :] for t in range(6)]
            dist_sq = jnp.maximum(geo[slot, base + k, here, 0:SLOTS], TINY)
            along = geo[slot, base + k, here, SLOTS : 2 * SLOTS]
            fall = jnp.maximum(1.0 - dist_sq * lax.rsqrt(dist_sq), 0.0)
            weight = fall * fall * fall * m
            closing = jnp.minimum(along, 0.0) / ((dist_sq + EPS) * (own_qs + q))
            push = weight * ((own_ts + term) - closing)
            sums[0] = sums[0] + push
            sums[1] = sums[1] + push * x0
            sums[2] = sums[2] + push * x1
            sums[3] = sums[3] + push * x2
            sums[4] = sums[4] + weight * along
        for t in range(5):
            acc[t, where, :] = sums[t]

    def both(ahead, ahead_groups, slot, groups):
        made = products(ahead, ahead_groups)
        units, base = [], 0
        for owns, nears in groups:
            for at in range(len(owns)):
                units += [(base, owns, nears, at, piece) for piece in range(0, SLOTS, CHUNK)]
            base += len(nears)
        share = len(units) // len(made)
        for at, make in enumerate(made):
            make()
            for base, owns, nears, which, piece in units[at * share : (at + 1) * share]:
                add_pairs(slot, base, owns, nears, which, piece)

    def run_class(steps, plan, hook=None):
        for make in products(0, plan(0)):
            make()

        def two(at, carry):
            step = 2 * at
            if hook is not None:
                hook(at)
            both(1, plan(step + 1), 0, plan(step))
            both(0, plan(jnp.minimum(step + 2, steps - 1)), 1, plan(step + 1))
            return carry

        lax.fori_loop(0, steps // 2, two, 0)

    def cell_at(cx, cy, cz):
        return cx * 16 + cy * 4 + cz

    def own_group(step):
        pair, side = step // 2, step % 2
        nears = [cell_at(1 + side, 1 + k // 2, 1 + k % 2) for k in range(4)]
        return [2 * pair, 2 * pair + 1], nears

    def pick(axis, values):
        if isinstance(axis, int):
            return values[axis]
        return jnp.where(axis == 0, values[0], jnp.where(axis == 1, values[1], values[2]))

    OWN, NEAR = (4, 2, 1), (16, 4, 1)

    def face_group(axis, side, which):
        low, high = pick(axis, (1, 0, 0)), pick(axis, (2, 2, 1))
        owns = [
            side * pick(axis, OWN) + which * pick(low, OWN) + last * pick(high, OWN) for last in range(2)
        ]
        nears = [
            side * 3 * pick(axis, NEAR) + (1 + k // 2) * pick(low, NEAR) + (1 + k % 2) * pick(high, NEAR)
            for k in range(4)
        ]
        return owns, nears

    def main_plan(step):
        face = step - 8
        axis = jnp.where(step < 12, 1, jnp.where(step < 16, 2, 0))
        inner = own_group(step)
        outer = face_group(axis, (face // 2) % 2, face % 2)
        return [
            tuple([jnp.where(step < 8, i, o) for i, o in zip(a, b)] for a, b in zip(inner, outer))
        ]

    def edge_plan(step):
        free, side = step // 2, step % 2
        low, high = pick(free, (1, 0, 0)), pick(free, (2, 2, 1))
        groups = []
        for other in range(2):
            owns = [
                side * pick(low, OWN) + other * pick(high, OWN) + last * pick(free, OWN)
                for last in range(2)
            ]
            nears = [
                side * 3 * pick(low, NEAR) + other * 3 * pick(high, NEAR) + (1 + last) * pick(free, NEAR)
                for last in range(2)
            ]
            groups.append((owns, nears))
        return groups

    def corner_plan(step):
        return [
            ([step * 4 + k], [cell_at(3 * step, 3 * (k // 2), 3 * (k % 2))]) for k in range(4)
        ]

    def build(phase, total, spot_of):
        def four(at, carry):
            for k in range(4):
                features(phase, *spot_of(4 * at + k))
            return carry

        lax.fori_loop(0, total // 4, four, 0)

    def face_spot(axis):
        others = [k for k in range(3) if k != axis]

        def spot(at):
            out = [None] * 3
            out[axis] = (at // 4) * 3
            out[others[0]], out[others[1]] = 1 + (at // 2) % 2, 1 + at % 2
            return out

        return spot

    def edge_spot(free):
        others = [k for k in range(3) if k != free]

        def spot(at):
            out = [None] * 3
            out[others[0]], out[others[1]], out[free] = (at // 4) * 3, ((at // 2) % 2) * 3, 1 + at % 2
            return out

        return spot

    def corner_spot(at):
        return [(at // 4) * 3, ((at // 2) % 2) * 3, (at % 2) * 3]

    def build_own(phase):
        def two(at, carry):
            for k in range(2):
                o = 2 * at + k
                features(phase, 1 + o // 4, 1 + (o // 2) % 2, 1 + o % 2, own=o)
            return carry

        lax.fori_loop(0, 4, two, 0)

    x_faces = [(-1, 0, 0), (1, 0, 0)]
    y_faces = [(0, -1, 0), (0, 1, 0)]
    z_faces = [(0, 0, -1), (0, 0, 1)]
    xy_edges = [r for r in REGIONS if r[0] and r[1] and not r[2]]
    xz_edges = [r for r in REGIONS if r[0] and not r[1] and r[2]]
    yz_edges = [r for r in REGIONS if not r[0] and r[1] and r[2]]
    corners = [r for r in REGIONS if r[0] and r[1] and r[2]]

    def rates(phase):
        def hook(at):
            @pl.when(at == 3)
            def _():
                wait_in(phase, y_faces)
                start(phase, yz_edges)
                build(phase, 8, face_spot(1))
                wait_in(phase, z_faces)
                build(phase, 8, face_spot(2))

            @pl.when(at == 7)
            def _():
                wait_in(phase, x_faces)
                start(phase, xy_edges + xz_edges)
                build(phase, 8, face_spot(0))

            @pl.when(at == 9)
            def _():
                wait_in(phase, xy_edges)
                start(phase, corners)

        run_class(20, main_plan, hook)
        wait_in(phase, yz_edges)
        build(phase, 8, edge_spot(0))
        build(phase, 8, edge_spot(2))
        wait_in(phase, xz_edges)
        build(phase, 8, edge_spot(1))
        run_class(6, edge_plan)
        wait_in(phase, corners)
        build(phase, 8, corner_spot)
        run_class(2, corner_plan)

    def own_rates(o, cx, cy, cz):
        rows = pl.ds(pl.multiple_of(o * SLOTS, SLOTS), SLOTS)
        column = lax.broadcasted_iota(jnp.int32, (SLOTS, SLOTS), 1)
        table = jnp.zeros((SLOTS, SLOTS), F32)
        for t in range(5):
            table = jnp.where(column == t, jnp.sum(acc[t, rows, :], axis=1, keepdims=True), table)
        sums = table.T[0:8]
        x = near_rows[cell_at(cx, cy, cz)][0:3]
        gravity = jnp.where(row == 2, 1.0, 0.0)[0:3]
        accel = GRADIENT * (x * sums[0:1] - sums[1:4]) - gravity
        return accel, -GRADIENT * sums[4:5]

    acc[...] = jnp.zeros_like(acc)
    for load in loads:
        load.wait()
    filled = []
    for o in range(8):
        y, z = (o // 2) % 2, o % 2
        filled.append(jnp.broadcast_to(occ_ref[o // 4][y : y + 1, z : z + 1], (1, SLOTS)))
    live = lane < jnp.concatenate(filled, 0)
    carried = jnp.where(live, mass_ref[...], 0.0)
    for which in (1, 2):
        chosen = jnp.logical_and(live, dir_ref[...] == which)
        code[which - 1] = jnp.where(chosen, slot_ref[...], -1)
    code[2] = jnp.where(jnp.logical_and(live, dir_ref[...] == 0), 1, 0)
    for o in range(8):
        cx, cy, cz = 1 + o // 4, 1 + (o // 2) % 2, 1 + o % 2
        first[cx, cy, cz] = jnp.concatenate(
            [off_ref[k, o : o + 1] for k in range(3)]
            + [vel_ref[k, o : o + 1] for k in range(3)]
            + [rho_ref[o : o + 1], carried[o : o + 1]],
            0,
        )

    slots = lax.broadcasted_iota(jnp.int32, (SLOTS, SLOTS), 0)
    for which in range(2):
        for o in range(8):
            target = jnp.broadcast_to(code[which, o : o + 1, :], (SLOTS, SLOTS))
            one_hot[which, :, o * SLOTS : (o + 1) * SLOTS] = jnp.where(slots == target, 1.0, 0.0).astype(BF16)
    build_own(0)
    pl.semaphore_wait(barrier, greeted)
    start(0, x_faces + y_faces + z_faces)
    rates(0)

    def to_half(o):
        cx, cy, cz = 1 + o // 4, 1 + (o // 2) % 2, 1 + o % 2
        accel, rate = own_rates(o, cx, cy, cz)
        tile = first[cx, cy, cz]
        half[cx, cy, cz] = jnp.concatenate(
            [tile[3:6] + HALF_STEP * accel, tile[6:7] + HALF_STEP * rate], 0
        )

    def over_own(update):
        def four(at, carry):
            for k in range(4):
                update(4 * at + k)
            return carry

        lax.fori_loop(0, 2, four, 0)

    over_own(to_half)
    start(1, x_faces + y_faces + z_faces)
    acc[...] = jnp.zeros_like(acc)
    build_own(1)
    rates(1)

    def to_new(o):
        cx, cy, cz = 1 + o // 4, 1 + (o // 2) % 2, 1 + o % 2
        accel, rate = own_rates(o, cx, cy, cz)
        tile = first[cx, cy, cz]
        new_pos = tile[0:3] + TIME_STEP * half[cx, cy, cz][0:3]
        new_vel = tile[3:6] + TIME_STEP * accel
        new_rho = tile[6:7] + TIME_STEP * rate
        new = jnp.concatenate([new_pos, new_vel, new_rho, jnp.zeros((1, SLOTS), F32)], 0)
        stays = jnp.broadcast_to(code[2, pl.ds(o, 1), :], (8, SLOTS)) > 0
        fresh[o] = jnp.where(stays, new, 0.0)
        spot = jnp.where(row == 0, cx - 1, jnp.where(row == 1, cy - 1, jnp.where(row == 2, cz - 1, 0)))
        record = new + spot.astype(F32)
        columns = pl.ds(pl.multiple_of(o * SLOTS, SLOTS), SLOTS)
        for which, by in ((0, -2.0), (1, 2.0)):
            parts = split3(record + jnp.where(row == 0, by, 0.0))
            stack = jnp.concatenate([*parts, jnp.zeros((8, SLOTS), F32)], 0)
            records[which, :, columns] = stack.astype(BF16)

    over_own(to_new)
    for which in range(2):
        found = lax.dot_general(
            records[which], one_hot[which], (((1,), (1,)), ((), ())), preferred_element_type=F32
        )
        lists[which] = (found[0:8] + found[8:16]) + found[16:24]

    def list_copy(which):
        step = 1 if which == 0 else -1
        other = lax.rem(place[0] + step + count[0], count[0])
        copy = pltpu.make_async_remote_copy(
            src_ref=lists.at[which],
            dst_ref=landed.at[which],
            send_sem=list_send.at[which],
            recv_sem=list_recv.at[which],
            device_id={"gx": other},
            device_id_type=MESH,
        )
        upper, lower = place[0] < count[0] - 1, place[0] > 0
        return copy, (upper, lower)[which], (lower, upper)[which]

    for which in range(2):
        copy, sends, _ = list_copy(which)

        @pl.when(sends)
        def _():
            copy.start()

    for o in range(8):
        tile = fresh[o]
        for k in range(3):
            pos_out[k, o : o + 1, :] = tile[k : k + 1]
            vel_out[k, o : o + 1, :] = tile[3 + k : 4 + k]
        rho_out[o : o + 1, :] = tile[6:7]
    wait_out(0, REGIONS)
    wait_out(1, REGIONS)
    for which in range(2):
        copy, sends, receives = list_copy(which)

        @pl.when(receives)
        def _():
            copy.wait_recv()

        @pl.when(sends)
        def _():
            copy.wait_send()

    for which in range(2):
        tile = landed[which]
        for k in range(7):
            arr_out[2 * k + which] = tile[k : k + 1]


def hand_over(*refs):
    given, results, sem = refs[:4], refs[4:8], refs[8]
    copies = [pltpu.make_async_copy(a, b, sem.at[at]) for at, (a, b) in enumerate(zip(given, results))]
    for copy in copies:
        copy.start()
    for copy in copies:
        copy.wait()


def body(offsets, velocity, density, mass, occupancy, move_direction, move_slot):
    vmem = pl.BlockSpec(memory_space=pltpu.VMEM)
    hbm = pl.BlockSpec(memory_space=pltpu.HBM)
    pos, vel, rho, arr = pl.pallas_call(
        kernel,
        out_shape=(
            jax.ShapeDtypeStruct((3, 8, SLOTS), F32),
            jax.ShapeDtypeStruct((3, 8, SLOTS), F32),
            jax.ShapeDtypeStruct((8, SLOTS), F32),
            jax.ShapeDtypeStruct((14, 1, SLOTS), F32),
        ),
        in_specs=[hbm] * 7,
        out_specs=(vmem, vmem, vmem, vmem),
        scratch_shapes=[
            pltpu.VMEM((3, 8, SLOTS), F32),
            pltpu.VMEM((3, 8, SLOTS), F32),
            pltpu.VMEM((8, SLOTS), F32),
            pltpu.VMEM((8, SLOTS), F32),
            pltpu.VMEM((2, 2, 2), jnp.int32),
            pltpu.VMEM((8, SLOTS), jnp.int32),
            pltpu.VMEM((8, SLOTS), jnp.int32),
            pltpu.VMEM((4, 4, 4, 8, SLOTS), F32),
            pltpu.VMEM((4, 4, 4, 4, SLOTS), F32),
            pltpu.VMEM((64, 64, 2 * SLOTS), BF16),
            pltpu.VMEM((8, SLOTS, 64), BF16),
            pltpu.VMEM((64, 8, SLOTS), F32),
            pltpu.VMEM((8 * SLOTS, SLOTS), F32),
            pltpu.VMEM((8 * SLOTS, SLOTS), F32),
            pltpu.VMEM((2, 4, 2 * SLOTS, 2 * SLOTS), F32),
            pltpu.VMEM((5, 8 * SLOTS, SLOTS), F32),
            pltpu.VMEM((3, 8, SLOTS), jnp.int32),
            pltpu.VMEM((8, 8, SLOTS), F32),
            pltpu.VMEM((2, 8, SLOTS), F32),
            pltpu.VMEM((2, 8, SLOTS), F32),
            pltpu.VMEM((2, 32, 8 * SLOTS), BF16),
            pltpu.VMEM((2, SLOTS, 8 * SLOTS), BF16),
            pltpu.SemaphoreType.DMA((7,)),
            pltpu.SemaphoreType.DMA((2, 26)),
            pltpu.SemaphoreType.DMA((2, 26)),
            pltpu.SemaphoreType.DMA((2,)),
            pltpu.SemaphoreType.DMA((2,)),
        ],
        compiler_params=pltpu.CompilerParams(
            collective_id=0, has_side_effects=True, vmem_limit_bytes=67_043_328
        ),
        name="sph_step",
    )(
        offsets.reshape(3, 8, SLOTS),
        velocity.reshape(3, 8, SLOTS),
        density.reshape(8, SLOTS),
        mass.reshape(8, SLOTS),
        occupancy,
        move_direction.reshape(8, SLOTS),
        move_slot.reshape(8, SLOTS),
    )
    pos, vel, rho, arr = pl.pallas_call(
        hand_over,
        out_shape=tuple(jax.ShapeDtypeStruct(a.shape, a.dtype) for a in (pos, vel, rho, arr)),
        in_specs=[vmem] * 4,
        out_specs=(pl.BlockSpec(memory_space=pltpu.HBM),) * 4,
        scratch_shapes=[pltpu.SemaphoreType.DMA((4,))],
        name="hand_over",
    )(pos, vel, rho, arr)
    return (
        pos.reshape(offsets.shape),
        vel.reshape(velocity.shape),
        rho.reshape(density.shape),
        arr.reshape(7, 2, 1, 1, 1, SLOTS),
    )


def solution(mesh):
    placed = (
        P(None, "gx", "gy", "gz", None),
        P(None, "gx", "gy", "gz", None),
        P("gx", "gy", "gz", None),
        P("gx", "gy", "gz", None),
        P("gx", "gy", "gz"),
        P("gx", "gy", "gz", None),
        P("gx", "gy", "gz", None),
    )
    return jax.shard_map(
        body,
        mesh=mesh,
        in_specs=placed,
        out_specs=(
            P(None, "gx", "gy", "gz", None),
            P(None, "gx", "gy", "gz", None),
            P("gx", "gy", "gz", None),
            P(None, None, "gx", "gy", "gz", None),
        ),
        check_vma=False,
    )
```

```python
import math

import jax
import jax.numpy as jnp
from jax import lax
from jax.experimental import pallas as pl
from jax.experimental.pallas import tpu as pltpu
from jax.sharding import PartitionSpec as P

F32 = jnp.float32
BF16 = jnp.bfloat16
MESH = pl.DeviceIdType.MESH
AXES = ("gx", "gy", "gz")
SLOTS = 128

SMOOTH = 0.5
KERNEL_NORM = 21.0 / (16.0 * math.pi * SMOOTH**3)
GRADIENT = 5.0 * KERNEL_NORM / SMOOTH**2
SOUND_SPEED = 10.0
STIFFNESS = SOUND_SPEED**2 / 7.0
TIME_STEP = 0.1
HALF_STEP = 0.05
EPS = 0.01 * SMOOTH * SMOOTH
TINY = 1e-12
CHUNK = 16

REGIONS = [
    (dx, dy, dz)
    for dx in (-1, 0, 1)
    for dy in (-1, 0, 1)
    for dz in (-1, 0, 1)
    if (dx, dy, dz) != (0, 0, 0)
]
SLOT_OF = {region: at for at, region in enumerate(REGIONS)}


def split3(value):
    first = value.astype(BF16).astype(F32)
    rest = value - first
    second = rest.astype(BF16).astype(F32)
    return first, second, rest - second


def row_iota():
    return lax.broadcasted_iota(jnp.int32, (8, SLOTS), 0)


def kernel(
    off_hbm, vel_hbm, rho_hbm, mass_hbm, occ_hbm, dir_hbm, slot_hbm,
    pos_out, vel_out, rho_out, arr_out,
    off_ref, vel_ref, rho_ref, mass_ref, occ_ref, dir_ref, slot_ref,
    first, half, near_feat, own_feat, near_rows, own_q, own_t, geo, acc, code, fresh, lists, landed,
    records, one_hot, load_sem, send_sem, recv_sem, list_send, list_recv,
):
    place = [lax.axis_index(axis) for axis in AXES]
    count = [lax.axis_size(axis) for axis in AXES]
    row = row_iota()
    lane = lax.broadcasted_iota(jnp.int32, (8, SLOTS), 1)

    sources = (off_hbm, vel_hbm, rho_hbm, mass_hbm, occ_hbm, dir_hbm, slot_hbm)
    held = (off_ref, vel_ref, rho_ref, mass_ref, occ_ref, dir_ref, slot_ref)
    loads = [
        pltpu.make_async_copy(source, target, load_sem.at[at])
        for at, (source, target) in enumerate(zip(sources, held))
    ]
    for load in loads:
        load.start()

    first[...] = jnp.zeros_like(first)
    half[...] = jnp.zeros_like(half)
    landed[...] = jnp.zeros_like(landed)

    barrier = pltpu.get_barrier_semaphore()
    greeted = jnp.int32(0)
    for at, axis in enumerate(AXES):
        for step in (-1, 1):
            other = place[at] + step
            there = jnp.logical_and(other >= 0, other < count[at])

            @pl.when(there)
            def _():
                pl.semaphore_signal(barrier, inc=1, device_id={axis: other}, device_id_type=MESH)

            greeted = greeted + there.astype(jnp.int32)

    def halo_copy(phase, region):
        at = max(k for k in range(3) if region[k] != 0)
        buffer = (first, half)[phase]
        source, target = [], []
        for k in range(3):
            span = {-1: 0, 0: pl.ds(1, 2), 1: 3}[region[k]]
            target.append(span)
            source.append({-1: 2, 1: 1}[region[k]] if k == at else span)
        other = lax.rem(place[at] - region[at] + count[at], count[at])
        copy = pltpu.make_async_remote_copy(
            src_ref=buffer.at[tuple(source)],
            dst_ref=buffer.at[tuple(target)],
            send_sem=send_sem.at[phase, SLOT_OF[region]],
            recv_sem=recv_sem.at[phase, SLOT_OF[region]],
            device_id={AXES[at]: other},
            device_id_type=MESH,
        )
        sends = place[at] < count[at] - 1 if region[at] < 0 else place[at] > 0
        receives = place[at] > 0 if region[at] < 0 else place[at] < count[at] - 1
        return copy, sends, receives

    def start(phase, regions):
        for region in regions:
            copy, sends, _ = halo_copy(phase, region)

            @pl.when(sends)
            def _():
                copy.start()

    def wait_in(phase, regions):
        for region in regions:
            copy, _, receives = halo_copy(phase, region)

            @pl.when(receives)
            def _():
                copy.wait_recv()

    def wait_out(phase, regions):
        for region in regions:
            copy, sends, _ = halo_copy(phase, region)

            @pl.when(sends)
            def _():
                copy.wait_send()

    def cell_tile(phase, cx, cy, cz):
        tile = first[cx, cy, cz]
        if phase == 0:
            return tile
        now = half[cx, cy, cz]
        return jnp.concatenate([tile[0:3] + HALF_STEP * tile[3:6], now, tile[7:8]], 0)

    def features(phase, cx, cy, cz, own=None):
        tile = cell_tile(phase, cx, cy, cz)
        shift = jnp.where(row == 0, cx, jnp.where(row == 1, cy, jnp.where(row == 2, cz, 2))) - 2
        moved = tile + shift.astype(F32)
        x, v, rho, m = moved[0:3], moved[3:6], moved[6:7], moved[7:8]
        norm = jnp.sum(x * x, axis=0, keepdims=True)
        cross = jnp.sum(x * v, axis=0, keepdims=True)
        parts = split3(jnp.concatenate([x, v, norm, cross], 0))
        zero = jnp.zeros((8, SLOTS), F32)
        dist, along = [], []
        for at, part in enumerate(parts):
            one = 1.0 if at == 0 else 0.0
            dist.append(jnp.where(row < 3, -2.0 * part, jnp.where(row == 6, one, 0.0)))
            swapped = jnp.concatenate([part[3:6], part[0:3], part[6:8]], 0)
            along.append(jnp.where(row < 6, -swapped, jnp.where(row == 7, one, 0.0)))
        pad = jnp.zeros((5, SLOTS), F32)
        dist_own = jnp.concatenate([part[6:7] for part in parts] + [pad], 0)
        along_own = jnp.concatenate([part[7:8] for part in parts] + [pad], 0)
        cell = cx * 16 + cy * 4 + cz
        for at, (blocks, last) in enumerate(((dist, dist_own), (along, along_own))):
            full = jnp.concatenate(
                [blocks[0], blocks[1], blocks[2], blocks[0], blocks[1], blocks[0], last, zero], 0
            )
            near_feat[cell, :, at * SLOTS : (at + 1) * SLOTS] = full.astype(BF16)
        q = jnp.where(m > 0, rho, 1.0)
        q2 = q * q
        term = STIFFNESS * (q2 * q2 * q2 * q - 1.0) / q2
        near_rows[cell] = jnp.concatenate([x, q, term, m, zero[0:2]], 0)
        if own is not None:
            a, b, c = parts
            ones = jnp.where(row < 3, 1.0, 0.0)
            extra = jnp.concatenate([q, term, zero[0:6]], 0)
            stack = jnp.concatenate([a, a, a, b, b, c, ones, extra], 0).T
            own_feat[own] = stack.astype(BF16)
            rows = pl.ds(pl.multiple_of(own * SLOTS, SLOTS), SLOTS)
            own_q[rows, :] = jnp.broadcast_to(stack[:, 56:57], (SLOTS, SLOTS))
            own_t[rows, :] = jnp.broadcast_to(stack[:, 57:58], (SLOTS, SLOTS))

    def products(slot, groups):
        made, at = [], 0
        for owns, nears in groups:
            for near in nears:

                def make(owns=owns, near=near, at=at):
                    left = own_feat[owns[0]]
                    if len(owns) > 1:
                        left = jnp.concatenate([own_feat[o] for o in owns], 0)
                    geo[slot, at, 0 : len(owns) * SLOTS, :] = jnp.dot(
                        left, near_feat[near], preferred_element_type=F32
                    )

                made.append(make)
                at += 1
        return made

    def add_pairs(slot, base, owns, nears, at, piece):
        o = owns[at]
        where = pl.ds(pl.multiple_of(o * SLOTS, SLOTS) + piece, CHUNK)
        here = slice(at * SLOTS + piece, at * SLOTS + piece + CHUNK)
        own_qs, own_ts = own_q[where, :], own_t[where, :]
        sums = [acc[t, where, :] for t in range(5)]
        for k, near in enumerate(nears):
            x0, x1, x2, q, term, m = [near_rows[near, pl.ds(t, CHUNK, stride=0), :] for t in range(6)]
            dist_sq = jnp.maximum(geo[slot, base + k, here, 0:SLOTS], TINY)
            along = geo[slot, base + k, here, SLOTS : 2 * SLOTS]
            fall = jnp.maximum(1.0 - dist_sq * lax.rsqrt(dist_sq), 0.0)
            weight = fall * fall * fall * m
            closing = jnp.minimum(along, 0.0) / ((dist_sq + EPS) * (own_qs + q))
            push = weight * ((own_ts + term) - closing)
            sums[0] = sums[0] + push
            sums[1] = sums[1] + push * x0
            sums[2] = sums[2] + push * x1
            sums[3] = sums[3] + push * x2
            sums[4] = sums[4] + weight * along
        for t in range(5):
            acc[t, where, :] = sums[t]

    def both(ahead, ahead_groups, slot, groups):
        made = products(ahead, ahead_groups)
        units, base = [], 0
        for owns, nears in groups:
            for at in range(len(owns)):
                units += [(base, owns, nears, at, piece) for piece in range(0, SLOTS, CHUNK)]
            base += len(nears)
        share = len(units) // len(made)
        for at, make in enumerate(made):
            make()
            for base, owns, nears, which, piece in units[at * share : (at + 1) * share]:
                add_pairs(slot, base, owns, nears, which, piece)

    def run_class(steps, plan, hook=None):
        for make in products(0, plan(0)):
            make()

        def two(at, carry):
            step = 2 * at
            if hook is not None:
                hook(at)
            both(1, plan(step + 1), 0, plan(step))
            both(0, plan(jnp.minimum(step + 2, steps - 1)), 1, plan(step + 1))
            return carry

        lax.fori_loop(0, steps // 2, two, 0)

    def cell_at(cx, cy, cz):
        return cx * 16 + cy * 4 + cz

    def own_group(step):
        pair, side = step // 2, step % 2
        nears = [cell_at(1 + side, 1 + k // 2, 1 + k % 2) for k in range(4)]
        return [2 * pair, 2 * pair + 1], nears

    def pick(axis, values):
        if isinstance(axis, int):
            return values[axis]
        return jnp.where(axis == 0, values[0], jnp.where(axis == 1, values[1], values[2]))

    OWN, NEAR = (4, 2, 1), (16, 4, 1)

    def face_group(axis, side, which):
        low, high = pick(axis, (1, 0, 0)), pick(axis, (2, 2, 1))
        owns = [
            side * pick(axis, OWN) + which * pick(low, OWN) + last * pick(high, OWN) for last in range(2)
        ]
        nears = [
            side * 3 * pick(axis, NEAR) + (1 + k // 2) * pick(low, NEAR) + (1 + k % 2) * pick(high, NEAR)
            for k in range(4)
        ]
        return owns, nears

    def main_plan(step):
        face = step - 8
        axis = jnp.where(step < 12, 1, jnp.where(step < 16, 2, 0))
        inner = own_group(step)
        outer = face_group(axis, (face // 2) % 2, face % 2)
        return [
            tuple([jnp.where(step < 8, i, o) for i, o in zip(a, b)] for a, b in zip(inner, outer))
        ]

    def edge_plan(step):
        free, side = step // 2, step % 2
        low, high = pick(free, (1, 0, 0)), pick(free, (2, 2, 1))
        groups = []
        for other in range(2):
            owns = [
                side * pick(low, OWN) + other * pick(high, OWN) + last * pick(free, OWN)
                for last in range(2)
            ]
            nears = [
                side * 3 * pick(low, NEAR) + other * 3 * pick(high, NEAR) + (1 + last) * pick(free, NEAR)
                for last in range(2)
            ]
            groups.append((owns, nears))
        return groups

    def corner_plan(step):
        return [
            ([step * 4 + k], [cell_at(3 * step, 3 * (k // 2), 3 * (k % 2))]) for k in range(4)
        ]

    def build(phase, total, spot_of):
        def four(at, carry):
            for k in range(4):
                features(phase, *spot_of(4 * at + k))
            return carry

        lax.fori_loop(0, total // 4, four, 0)

    def face_spot(axis):
        others = [k for k in range(3) if k != axis]

        def spot(at):
            out = [None] * 3
            out[axis] = (at // 4) * 3
            out[others[0]], out[others[1]] = 1 + (at // 2) % 2, 1 + at % 2
            return out

        return spot

    def edge_spot(free):
        others = [k for k in range(3) if k != free]

        def spot(at):
            out = [None] * 3
            out[others[0]], out[others[1]], out[free] = (at // 4) * 3, ((at // 2) % 2) * 3, 1 + at % 2
            return out

        return spot

    def corner_spot(at):
        return [(at // 4) * 3, ((at // 2) % 2) * 3, (at % 2) * 3]

    def build_own(phase):
        def two(at, carry):
            for k in range(4):
                o = 4 * at + k
                features(phase, 1 + o // 4, 1 + (o // 2) % 2, 1 + o % 2, own=o)
            return carry

        lax.fori_loop(0, 2, two, 0)

    x_faces = [(-1, 0, 0), (1, 0, 0)]
    y_faces = [(0, -1, 0), (0, 1, 0)]
    z_faces = [(0, 0, -1), (0, 0, 1)]
    xy_edges = [r for r in REGIONS if r[0] and r[1] and not r[2]]
    xz_edges = [r for r in REGIONS if r[0] and not r[1] and r[2]]
    yz_edges = [r for r in REGIONS if not r[0] and r[1] and r[2]]
    corners = [r for r in REGIONS if r[0] and r[1] and r[2]]

    def rates(phase):
        def hook(at):
            @pl.when(at == 3)
            def _():
                wait_in(phase, y_faces)
                start(phase, yz_edges)
                build(phase, 8, face_spot(1))
                wait_in(phase, z_faces)
                build(phase, 8, face_spot(2))

            @pl.when(at == 7)
            def _():
                wait_in(phase, x_faces)
                start(phase, xy_edges + xz_edges)
                build(phase, 8, face_spot(0))

            @pl.when(at == 9)
            def _():
                wait_in(phase, xy_edges)
                start(phase, corners)

        run_class(20, main_plan, hook)
        wait_in(phase, yz_edges)
        build(phase, 8, edge_spot(0))
        build(phase, 8, edge_spot(2))
        wait_in(phase, xz_edges)
        build(phase, 8, edge_spot(1))
        run_class(6, edge_plan)
        wait_in(phase, corners)
        build(phase, 8, corner_spot)
        run_class(2, corner_plan)

    def own_rates(o, cx, cy, cz):
        rows = pl.ds(pl.multiple_of(o * SLOTS, SLOTS), SLOTS)
        column = lax.broadcasted_iota(jnp.int32, (SLOTS, SLOTS), 1)
        table = jnp.zeros((SLOTS, SLOTS), F32)
        for t in range(5):
            table = jnp.where(column == t, jnp.sum(acc[t, rows, :], axis=1, keepdims=True), table)
        sums = table.T[0:8]
        x = near_rows[cell_at(cx, cy, cz)][0:3]
        gravity = jnp.where(row == 2, 1.0, 0.0)[0:3]
        accel = GRADIENT * (x * sums[0:1] - sums[1:4]) - gravity
        return accel, -GRADIENT * sums[4:5]

    acc[...] = jnp.zeros_like(acc)
    for load in loads:
        load.wait()
    filled = []
    for o in range(8):
        y, z = (o // 2) % 2, o % 2
        filled.append(jnp.broadcast_to(occ_ref[o // 4][y : y + 1, z : z + 1], (1, SLOTS)))
    live = lane < jnp.concatenate(filled, 0)
    carried = jnp.where(live, mass_ref[...], 0.0)
    for which in (1, 2):
        chosen = jnp.logical_and(live, dir_ref[...] == which)
        code[which - 1] = jnp.where(chosen, slot_ref[...], -1)
    code[2] = jnp.where(jnp.logical_and(live, dir_ref[...] == 0), 1, 0)
    for o in range(8):
        cx, cy, cz = 1 + o // 4, 1 + (o // 2) % 2, 1 + o % 2
        first[cx, cy, cz] = jnp.concatenate(
            [off_ref[k, o : o + 1] for k in range(3)]
            + [vel_ref[k, o : o + 1] for k in range(3)]
            + [rho_ref[o : o + 1], carried[o : o + 1]],
            0,
        )

    slots = lax.broadcasted_iota(jnp.int32, (SLOTS, SLOTS), 0)
    for which in range(2):
        for o in range(8):
            target = jnp.broadcast_to(code[which, o : o + 1, :], (SLOTS, SLOTS))
            one_hot[which, :, o * SLOTS : (o + 1) * SLOTS] = jnp.where(slots == target, 1.0, 0.0).astype(BF16)
    build_own(0)
    pl.semaphore_wait(barrier, greeted)
    start(0, x_faces + y_faces + z_faces)
    rates(0)

    def to_half(o):
        cx, cy, cz = 1 + o // 4, 1 + (o // 2) % 2, 1 + o % 2
        accel, rate = own_rates(o, cx, cy, cz)
        tile = first[cx, cy, cz]
        half[cx, cy, cz] = jnp.concatenate(
            [tile[3:6] + HALF_STEP * accel, tile[6:7] + HALF_STEP * rate], 0
        )

    def over_own(update):
        def four(at, carry):
            for k in range(4):
                update(4 * at + k)
            return carry

        lax.fori_loop(0, 2, four, 0)

    over_own(to_half)
    start(1, x_faces + y_faces + z_faces)
    acc[...] = jnp.zeros_like(acc)
    build_own(1)
    rates(1)

    def to_new(o):
        cx, cy, cz = 1 + o // 4, 1 + (o // 2) % 2, 1 + o % 2
        accel, rate = own_rates(o, cx, cy, cz)
        tile = first[cx, cy, cz]
        new_pos = tile[0:3] + TIME_STEP * half[cx, cy, cz][0:3]
        new_vel = tile[3:6] + TIME_STEP * accel
        new_rho = tile[6:7] + TIME_STEP * rate
        new = jnp.concatenate([new_pos, new_vel, new_rho, jnp.zeros((1, SLOTS), F32)], 0)
        stays = jnp.broadcast_to(code[2, pl.ds(o, 1), :], (8, SLOTS)) > 0
        fresh[o] = jnp.where(stays, new, 0.0)
        spot = jnp.where(row == 0, cx - 1, jnp.where(row == 1, cy - 1, jnp.where(row == 2, cz - 1, 0)))
        record = new + spot.astype(F32)
        columns = pl.ds(pl.multiple_of(o * SLOTS, SLOTS), SLOTS)
        for which, by in ((0, -2.0), (1, 2.0)):
            parts = split3(record + jnp.where(row == 0, by, 0.0))
            stack = jnp.concatenate([*parts, jnp.zeros((8, SLOTS), F32)], 0)
            records[which, :, columns] = stack.astype(BF16)

    over_own(to_new)
    for which in range(2):
        found = lax.dot_general(
            records[which], one_hot[which], (((1,), (1,)), ((), ())), preferred_element_type=F32
        )
        lists[which] = (found[0:8] + found[8:16]) + found[16:24]

    def list_copy(which):
        step = 1 if which == 0 else -1
        other = lax.rem(place[0] + step + count[0], count[0])
        copy = pltpu.make_async_remote_copy(
            src_ref=lists.at[which],
            dst_ref=landed.at[which],
            send_sem=list_send.at[which],
            recv_sem=list_recv.at[which],
            device_id={"gx": other},
            device_id_type=MESH,
        )
        upper, lower = place[0] < count[0] - 1, place[0] > 0
        return copy, (upper, lower)[which], (lower, upper)[which]

    for which in range(2):
        copy, sends, _ = list_copy(which)

        @pl.when(sends)
        def _():
            copy.start()

    for o in range(8):
        tile = fresh[o]
        for k in range(3):
            pos_out[k, o : o + 1, :] = tile[k : k + 1]
            vel_out[k, o : o + 1, :] = tile[3 + k : 4 + k]
        rho_out[o : o + 1, :] = tile[6:7]
    wait_out(0, REGIONS)
    wait_out(1, REGIONS)
    for which in range(2):
        copy, sends, receives = list_copy(which)

        @pl.when(receives)
        def _():
            copy.wait_recv()

        @pl.when(sends)
        def _():
            copy.wait_send()

    for which in range(2):
        tile = landed[which]
        for k in range(7):
            arr_out[2 * k + which] = tile[k : k + 1]


def hand_over(*refs):
    given, results, sem = refs[:4], refs[4:8], refs[8]
    copies = [pltpu.make_async_copy(a, b, sem.at[at]) for at, (a, b) in enumerate(zip(given, results))]
    for copy in copies:
        copy.start()
    for copy in copies:
        copy.wait()


def body(offsets, velocity, density, mass, occupancy, move_direction, move_slot):
    vmem = pl.BlockSpec(memory_space=pltpu.VMEM)
    hbm = pl.BlockSpec(memory_space=pltpu.HBM)
    pos, vel, rho, arr = pl.pallas_call(
        kernel,
        out_shape=(
            jax.ShapeDtypeStruct((3, 8, SLOTS), F32),
            jax.ShapeDtypeStruct((3, 8, SLOTS), F32),
            jax.ShapeDtypeStruct((8, SLOTS), F32),
            jax.ShapeDtypeStruct((14, 1, SLOTS), F32),
        ),
        in_specs=[hbm] * 7,
        out_specs=(vmem, vmem, vmem, vmem),
        scratch_shapes=[
            pltpu.VMEM((3, 8, SLOTS), F32),
            pltpu.VMEM((3, 8, SLOTS), F32),
            pltpu.VMEM((8, SLOTS), F32),
            pltpu.VMEM((8, SLOTS), F32),
            pltpu.VMEM((2, 2, 2), jnp.int32),
            pltpu.VMEM((8, SLOTS), jnp.int32),
            pltpu.VMEM((8, SLOTS), jnp.int32),
            pltpu.VMEM((4, 4, 4, 8, SLOTS), F32),
            pltpu.VMEM((4, 4, 4, 4, SLOTS), F32),
            pltpu.VMEM((64, 64, 2 * SLOTS), BF16),
            pltpu.VMEM((8, SLOTS, 64), BF16),
            pltpu.VMEM((64, 8, SLOTS), F32),
            pltpu.VMEM((8 * SLOTS, SLOTS), F32),
            pltpu.VMEM((8 * SLOTS, SLOTS), F32),
            pltpu.VMEM((2, 4, 2 * SLOTS, 2 * SLOTS), F32),
            pltpu.VMEM((5, 8 * SLOTS, SLOTS), F32),
            pltpu.VMEM((3, 8, SLOTS), jnp.int32),
            pltpu.VMEM((8, 8, SLOTS), F32),
            pltpu.VMEM((2, 8, SLOTS), F32),
            pltpu.VMEM((2, 8, SLOTS), F32),
            pltpu.VMEM((2, 32, 8 * SLOTS), BF16),
            pltpu.VMEM((2, SLOTS, 8 * SLOTS), BF16),
            pltpu.SemaphoreType.DMA((7,)),
            pltpu.SemaphoreType.DMA((2, 26)),
            pltpu.SemaphoreType.DMA((2, 26)),
            pltpu.SemaphoreType.DMA((2,)),
            pltpu.SemaphoreType.DMA((2,)),
        ],
        compiler_params=pltpu.CompilerParams(
            collective_id=0, has_side_effects=True, vmem_limit_bytes=67_043_328
        ),
        name="sph_step",
    )(
        offsets.reshape(3, 8, SLOTS),
        velocity.reshape(3, 8, SLOTS),
        density.reshape(8, SLOTS),
        mass.reshape(8, SLOTS),
        occupancy,
        move_direction.reshape(8, SLOTS),
        move_slot.reshape(8, SLOTS),
    )
    pos, vel, rho, arr = pl.pallas_call(
        hand_over,
        out_shape=tuple(jax.ShapeDtypeStruct(a.shape, a.dtype) for a in (pos, vel, rho, arr)),
        in_specs=[vmem] * 4,
        out_specs=(pl.BlockSpec(memory_space=pltpu.HBM),) * 4,
        scratch_shapes=[pltpu.SemaphoreType.DMA((4,))],
        name="hand_over",
    )(pos, vel, rho, arr)
    return (
        pos.reshape(offsets.shape),
        vel.reshape(velocity.shape),
        rho.reshape(density.shape),
        arr.reshape(7, 2, 1, 1, 1, SLOTS),
    )


def solution(mesh):
    placed = (
        P(None, "gx", "gy", "gz", None),
        P(None, "gx", "gy", "gz", None),
        P("gx", "gy", "gz", None),
        P("gx", "gy", "gz", None),
        P("gx", "gy", "gz"),
        P("gx", "gy", "gz", None),
        P("gx", "gy", "gz", None),
    )
    return jax.shard_map(
        body,
        mesh=mesh,
        in_specs=placed,
        out_specs=(
            P(None, "gx", "gy", "gz", None),
            P(None, "gx", "gy", "gz", None),
            P("gx", "gy", "gz", None),
            P(None, None, "gx", "gy", "gz", None),
        ),
        check_vma=False,
    )
```
